256 devices in a mesh: row: 32 (over x, y, core), col: 8 (over z).
Axes of the slice: x: 4, y: 4, z: 8, core: 2. Of those that a mesh axis runs over, the one named last changes fastest.
Arguments:
- blocks: float32 [32, 8, 8, 32, 2, 8, 128], P('row', 'col'), may hold values from 0.5 to 1620
- plan: int32 [32, 8, 8, 32, 2], P('row', 'col'), may hold values from 0 to 4095, as said below
- live: int32 [32, 8, 8, 32], P('row', 'col'), may hold values from 1 to 2, as said below
- row_emb: float32 [300, 32768], P(None, ('row', 'col')), may hold values from -1.5 to 1.5
- col_emb: float32 [300, 32768], P(None, ('col', 'row')), may hold values from -1.5 to 1.5
- row_acc: float32 [300, 32768], P(None, ('row', 'col')), may hold values from 0.5 to 5
- col_acc: float32 [300, 32768], P(None, ('col', 'row')), may hold values from 0.5 to 5
Outputs:
- new_row_emb: float32 [300, 32768], P(None, ('row', 'col'))
- new_col_emb: float32 [300, 32768], P(None, ('col', 'row'))
- new_row_acc: float32 [300, 32768], P(None, ('row', 'col'))
- new_col_acc: float32 [300, 32768], P(None, ('col', 'row'))
The draws below stay inside these ranges and needn't reach their ends.
Inputs may be any that keep to these rules, and one draw needn't show every extreme that they name: plan[r, c, c2, r2, p] is a sub-block number of tile (r, c); numbers may repeat and repeated slots add. Over all index pairs (r2, c2), slot 0 names every sub-block row and every sub-block column of each tile. Slots at or past live[r, c, c2, r2] hold values that are not counts. In every draw some tile gets 2 live slots from every index pair.
All inputs are finite; a program needn't handle non-finite values.
Results may differ from the reference program's by a relative error of at most 0.0003.
Values sent between devices are 32-bit elements; how exact they have to be, the bound alone decides.
No kernel may reach another device: no remote copies, remote signals or barrier semaphores. Data moves between devices by JAX's collectives and lax.ppermute only.
A program may use at most 192 MiB of HBM per device.

```python
import math
import jax
import jax.numpy as jnp
from jax import lax

DIM = 300
TILE_WORD_ROWS = 1024
TILE_WORD_COLUMNS = 4096
SUBBLOCK_COLUMNS = 128
SUBBLOCK_ROWS = 8
SLOTS_PER_DEVICE = 2
ROWS = 32768
COLS = 32768
N_ROW = 32
N_COL = 8


def draw_blocks(key, part):
    complete_shape = (N_ROW, N_COL, N_COL, N_ROW, SLOTS_PER_DEVICE, SUBBLOCK_ROWS, SUBBLOCK_COLUMNS)
    col_rise = 1.0 + 2.0 * lax.broadcasted_iota(jnp.float32, complete_shape, 2) / max(N_COL - 1, 1)
    row_rise = 1.0 + 2.0 * lax.broadcasted_iota(jnp.float32, complete_shape, 3) / max(N_ROW - 1, 1)
    subkey = jax.random.fold_in(key, 5)
    values = jnp.exp(jax.random.uniform(subkey, complete_shape, jnp.float32, math.log(0.5), math.log(20.0)))
    return values * col_rise * row_rise


def draw_plan(key, part):
    complete_shape = (N_ROW, N_COL, N_COL, N_ROW, SLOTS_PER_DEVICE)
    grid_row_count = TILE_WORD_ROWS // SUBBLOCK_ROWS
    grid_column_count = TILE_WORD_COLUMNS // SUBBLOCK_COLUMNS
    owners = N_ROW * N_COL
    key_any, key_rows, key_cols = jax.random.split(jax.random.fold_in(key, 11), 3)
    anywhere = jax.random.randint(key_any, complete_shape, 0, grid_row_count * grid_column_count, dtype=jnp.int32)
    rows_perm = jax.vmap(lambda subkey: jax.random.permutation(subkey, owners))(jax.random.split(key_rows, owners))
    cols_perm = jax.vmap(lambda subkey: jax.random.permutation(subkey, owners))(jax.random.split(key_cols, owners))
    first_slot = (rows_perm % grid_row_count * grid_column_count + cols_perm % grid_column_count).astype(jnp.int32)
    first_slot = first_slot.reshape(N_ROW, N_COL, N_COL, N_ROW)
    return jnp.concatenate([first_slot[..., None], anywhere[..., 1:]], axis=-1)


def draw_live(key, part):
    complete_shape = (N_ROW, N_COL, N_COL, N_ROW)
    key_base, key_pick = jax.random.split(jax.random.fold_in(key, 23))
    counts_base = jax.random.randint(key_base, complete_shape, 1, SLOTS_PER_DEVICE + 1, dtype=jnp.int32)
    chosen = jax.random.randint(key_pick, (), 0, N_ROW * N_COL, dtype=jnp.int32)
    owner_ids = lax.broadcasted_iota(jnp.int32, complete_shape, 0) * N_COL + lax.broadcasted_iota(jnp.int32, complete_shape, 1)
    return jnp.where(owner_ids == chosen, SLOTS_PER_DEVICE, counts_base).astype(jnp.int32)


def shard_levels(own_key, dims, cuts, smallest, top_value):
    def one(position, blocks):
        draws = jax.random.uniform(jax.random.fold_in(jax.random.fold_in(own_key, 6), position), (blocks,), jnp.float32, smallest / len(cuts), top_value / len(cuts))
        return jnp.repeat(jnp.exp(draws), dims[position] // blocks).reshape((-1,) + (1,) * (len(dims) - position - 1))

    loudness = one(*cuts[0])
    for cut in cuts[1:]:
        loudness = loudness * one(*cut)
    return loudness


def noise(own_key, shape, scale, reach, pieces=(), held_as=jnp.bfloat16):
    drawn = scale * jax.random.normal(own_key, shape, jnp.float32)
    if pieces:
        drawn = drawn * shard_levels(own_key, shape, pieces, -0.22, 0.18)
    return jnp.clip(drawn, -reach, reach).astype(held_as)


def setup_inputs(seed: int = 0) -> dict:
    splits = jax.random.split(jax.random.key(seed), 8)
    return {
        "blocks": draw_blocks(jax.random.fold_in(splits[7], 71), 0),
        "plan": draw_plan(jax.random.fold_in(splits[7], 71), 0),
        "live": draw_live(jax.random.fold_in(splits[7], 71), 0),
        "row_emb": noise(splits[3], (DIM, ROWS), 0.25, 1.5, ((1, 256),), jnp.float32),
        "col_emb": noise(splits[4], (DIM, COLS), 0.25, 1.5, ((1, 256),), jnp.float32),
        "row_acc": jnp.clip(jnp.exp(math.log(5.0) - 2.3025851 * jax.random.uniform(splits[5], (DIM, ROWS), jnp.float32) ** shard_levels(splits[5], (DIM, ROWS), ((1, 256),), -0.2, 0.2)), 0.5, 5.0),
        "col_acc": jnp.clip(jnp.exp(math.log(5.0) - 2.3025851 * jax.random.uniform(splits[6], (DIM, COLS), jnp.float32) ** shard_levels(splits[6], (DIM, COLS), ((1, 256),), -0.2, 0.2)), 0.5, 5.0),
    }


LEARNING_RATE = 0.2

def owner_tile(blocks, plan, live, row_index, col_index):
    slot_entries = jnp.swapaxes(blocks[:, :, col_index, row_index], 0, 1)
    places = plan[row_index, col_index]
    limits = live[row_index, col_index]
    slot_ids = lax.broadcasted_iota(jnp.int32, places.shape, 2)
    grid_row_count = TILE_WORD_ROWS // SUBBLOCK_ROWS
    grid_column_count = TILE_WORD_COLUMNS // SUBBLOCK_COLUMNS
    block_total = grid_row_count * grid_column_count
    target = jnp.where(slot_ids < limits[:, :, None], places, block_total).astype(jnp.int32)
    flat_layout = slot_entries.reshape(-1, SUBBLOCK_ROWS * SUBBLOCK_COLUMNS)
    dense_block_matrix = jax.ops.segment_sum(flat_layout, target.reshape(-1), num_segments=block_total + 1)[:block_total]
    return dense_block_matrix.reshape(grid_row_count, grid_column_count, SUBBLOCK_ROWS, SUBBLOCK_COLUMNS).transpose(0, 2, 1, 3).reshape(TILE_WORD_ROWS, TILE_WORD_COLUMNS)

def reference(blocks, plan, live, row_emb, col_emb, row_acc, col_acc):
    tile_ids = jnp.arange(N_ROW * N_COL, dtype=jnp.int32)
    highest = lax.Precision.HIGHEST

    def partial_sums(tile_id):
        tile_counts = owner_tile(blocks, plan, live, tile_id // N_COL, tile_id % N_COL)
        return (lax.optimization_barrier(jnp.sum(tile_counts, axis=1)), lax.optimization_barrier(jnp.sum(tile_counts, axis=0)))
    row_parts, col_parts = lax.map(partial_sums, tile_ids)
    row_mass = lax.optimization_barrier(jnp.sum(row_parts.reshape(N_ROW, N_COL, TILE_WORD_ROWS), axis=1))
    col_mass = lax.optimization_barrier(jnp.sum(col_parts.reshape(N_ROW, N_COL, TILE_WORD_COLUMNS), axis=0))
    grand_total = jnp.sum(row_mass)
    loss_scale = 4.0 * float(ROWS * COLS) ** (-0.25)

    def accumulate(totals, tile_id):
        row_grad, col_grad = totals
        row_index = tile_id // N_COL
        col_index = tile_id % N_COL
        tile_counts = owner_tile(blocks, plan, live, row_index, col_index)
        row_block = lax.dynamic_slice_in_dim(row_emb, row_index * TILE_WORD_ROWS, TILE_WORD_ROWS, 1)
        col_block = lax.dynamic_slice_in_dim(col_emb, col_index * TILE_WORD_COLUMNS, TILE_WORD_COLUMNS, 1)
        scores = jnp.dot(row_block.T, col_block, precision=highest)
        baseline = jnp.log(grand_total) - jnp.log(row_mass[row_index])[:, None] - jnp.log(col_mass[col_index])[None, :]
        positive = tile_counts > 0
        pmi_target = jnp.log(jnp.where(positive, tile_counts, 1.0)) + baseline
        confidence = 0.1 + 0.25 * jnp.sqrt(tile_counts)
        loss_grad = jnp.where(positive, confidence * (scores - pmi_target), jax.nn.sigmoid(scores - baseline)) * loss_scale
        row_term = jnp.dot(col_block, loss_grad.T, precision=highest)
        col_term = jnp.dot(row_block, loss_grad, precision=highest)
        row_old = lax.dynamic_slice_in_dim(row_grad, row_index * TILE_WORD_ROWS, TILE_WORD_ROWS, 1)
        col_old = lax.dynamic_slice_in_dim(col_grad, col_index * TILE_WORD_COLUMNS, TILE_WORD_COLUMNS, 1)
        row_grad = lax.dynamic_update_slice_in_dim(row_grad, row_old + row_term, row_index * TILE_WORD_ROWS, 1)
        col_grad = lax.dynamic_update_slice_in_dim(col_grad, col_old + col_term, col_index * TILE_WORD_COLUMNS, 1)
        return ((row_grad, col_grad), None)
    start = (jnp.zeros((DIM, ROWS), jnp.float32), jnp.zeros((DIM, COLS), jnp.float32))
    (row_grad, col_grad), _ = lax.scan(accumulate, start, tile_ids)
    new_row_acc = row_acc + row_grad * row_grad
    new_col_acc = col_acc + col_grad * col_grad
    new_row_emb = row_emb - LEARNING_RATE * row_grad / jnp.sqrt(new_row_acc)
    new_col_emb = col_emb - LEARNING_RATE * col_grad / jnp.sqrt(new_col_acc)
    return (new_row_emb, new_col_emb, new_row_acc, new_col_acc)
```

```python
import jax
import jax.numpy as jnp
from jax import lax
from jax.experimental import pallas as pl
from jax.experimental.pallas import tpu as pltpu
from jax.sharding import Mesh, PartitionSpec as P

LEARNING_RATE = 0.2
GRID_X, GRID_Y, CORES = 4, 4, 2
ROW = ("x", "y", "core")
ALL = ("col", "x", "y", "core")
LANES = 128
F32 = jnp.float32
BF16 = jnp.bfloat16


def split(value):
    high = value.astype(BF16)
    return high, (value - high.astype(F32)).astype(BF16)


def place_kernel(target, alive, arrived, counts_out, mass_out, dense, row_sums, col_sums):
    slots = arrived.shape[0]
    columns = col_sums.shape[0]
    row_words = row_sums.shape[0] // LANES * 8
    row_sums[...] = jnp.zeros(row_sums.shape, F32)
    col_sums[...] = jnp.zeros(col_sums.shape, F32)
    blank = jnp.zeros(arrived.shape[1:], F32)

    def clear(p, carry):
        dense[target[p]] = blank
        return carry

    lax.fori_loop(0, slots, clear, 0, unroll=8)

    def add(p, carry):
        place = target[p]
        value = jnp.where(alive[p] > 0, arrived[p], 0.0)
        dense[place] = dense[place] + value
        row_sums[place // columns] = row_sums[place // columns] + value
        col_sums[place % columns] = col_sums[place % columns] + value
        return carry

    lax.fori_loop(0, slots, add, 0, unroll=4)

    def read(p, carry):
        counts_out[p] = dense[target[p]]
        return carry

    lax.fori_loop(0, slots, read, 0, unroll=8)
    col_part = jnp.sum(col_sums[...], axis=1)
    mass_out[0:columns, :] = col_part
    ones = jnp.ones((8, LANES), F32)
    row_part = lax.dot_general(
        ones,
        row_sums[...].reshape(-1, LANES),
        (((1,), (1,)), ((), ())),
        precision=lax.Precision.HIGHEST,
        preferred_element_type=F32,
    )
    for i in range(row_words):
        mass_out[columns + i : columns + i + 1, :] = row_part[0:1, i * LANES : (i + 1) * LANES]
    mass_out[columns + row_words :, :] = jnp.full((8, LANES), jnp.sum(col_part), F32)


def place(target, alive, arrived, grid_rows, grid_columns):
    slots = arrived.shape[0]
    return pl.pallas_call(
        place_kernel,
        name="place_counts",
        grid_spec=pltpu.PrefetchScalarGridSpec(
            num_scalar_prefetch=2,
            grid=(1,),
            in_specs=[pl.BlockSpec(memory_space=pltpu.VMEM)],
            out_specs=[pl.BlockSpec(memory_space=pltpu.VMEM)] * 2,
            scratch_shapes=[
                pltpu.VMEM((grid_rows * grid_columns, 8, LANES), F32),
                pltpu.VMEM((grid_rows, 8, LANES), F32),
                pltpu.VMEM((grid_columns, 8, LANES), F32),
            ],
        ),
        out_shape=[
            jax.ShapeDtypeStruct((slots, 8, LANES), F32),
            jax.ShapeDtypeStruct((grid_columns + grid_rows * 8 // LANES + 8, LANES), F32),
        ],
        compiler_params=pltpu.CompilerParams(vmem_limit_bytes=40 << 20),
    )(target, alive, arrived)


def grad_kernel(
    target, core, row_blocks, col_blocks, counts, masses,
    row_term, col_term,
    scores, col_stack, row_stack, row_turned, row_bias, col_bias, fresh,
):
    n_row, dim, _ = row_blocks.shape
    n_col = col_blocks.shape[0]
    slots = counts.shape[0]
    deep = col_stack.shape[0]
    tile_rows = n_row * LANES
    chunk = 512
    per_chunk = chunk // LANES
    n_chunks = n_col // per_chunk
    row_tile = 256

    log_total = jnp.log(masses[n_col + n_row : n_col + n_row + 1, :])
    col_bias[...] = 0.5 * (jnp.log(masses[0:n_col, :]) - log_total)
    row_logs = 0.5 * jnp.log(masses[n_col : n_col + n_row, :])
    col_stack[3 * dim :, :] = jnp.zeros((deep - 3 * dim, n_col * LANES), BF16)

    def load_col(j, carry):
        high, low = split(col_blocks[j])
        here = pl.ds(pl.multiple_of(j * LANES, LANES), LANES)
        col_stack[0:dim, here] = high
        col_stack[dim : 2 * dim, here] = low
        col_stack[2 * dim : 3 * dim, here] = high
        return carry

    lax.fori_loop(0, n_col, load_col, 0)
    for i in range(n_row):
        value = row_blocks[i]
        high, low = split(value)
        here = slice(i * LANES, (i + 1) * LANES)
        row_stack[0:dim, here] = high
        row_stack[dim : 2 * dim, here] = low
        high32, low32 = high.astype(F32), low.astype(F32)
        tall = jnp.concatenate(
            [high32, high32, low32, jnp.zeros((deep - 3 * dim, LANES), F32)], axis=0
        )
        row_turned[here, :] = (0.5 * tall.T).astype(BF16)
        row_bias[here, :] = jnp.broadcast_to(row_logs[i : i + 1, :], (LANES, LANES)).T

    def score(step, carry):
        rt = step // n_chunks
        ct = step % n_chunks
        rows = pl.ds(pl.multiple_of(rt * row_tile, row_tile), row_tile)
        cols = pl.ds(pl.multiple_of(ct * chunk, chunk), chunk)
        product = jnp.dot(row_turned[rows, :], col_stack[:, cols], preferred_element_type=F32)
        bias = row_bias[rows, :]
        for k in range(per_chunk):
            out = product[:, k * LANES : (k + 1) * LANES] + bias + col_bias[pl.ds(ct * per_chunk + k, 1), :]
            scores[rows, pl.ds(pl.multiple_of(ct * chunk + k * LANES, LANES), LANES)] = out
        return carry

    lax.fori_loop(0, n_chunks * (tile_rows // row_tile), score, 0)

    def spot(p):
        where = target[p]
        return (
            pl.ds(pl.multiple_of(where // n_col * 8, 8), 8),
            pl.ds(pl.multiple_of(where % n_col * LANES, LANES), LANES),
        )

    def counted(p, carry):
        count = counts[p]
        fresh[p] = (0.1 + 0.25 * jnp.sqrt(count)) * (2.0 * scores[spot(p)] - jnp.log(count))
        return carry

    lax.fori_loop(0, slots, counted, 0, unroll=8)

    def smooth(step, carry):
        rows = pl.ds(pl.multiple_of(step * 32, 32), 32)
        scores[rows, :] = 0.5 * jnp.tanh(scores[rows, :]) + 0.5
        return carry

    lax.fori_loop(0, tile_rows // 32, smooth, 0)

    def put(p, carry):
        scores[spot(p)] = fresh[p]
        return carry

    lax.fori_loop(0, slots, put, 0, unroll=8)

    for i in range(n_row):
        row_term[i] = jnp.zeros((dim, LANES), F32)

    def grads(ct, carry):
        cols = pl.ds(pl.multiple_of(ct * chunk, chunk), chunk)
        high, low = split(scores[:, cols])
        both = jnp.dot(row_stack[...], high, preferred_element_type=F32)
        rest = jnp.dot(row_stack[0:dim, :], low, preferred_element_type=F32)
        total = both[0:dim] + both[dim:] + rest
        for k in range(per_chunk):
            j = ct * per_chunk + k
            col_term[(j % 2) ^ core[0], j // 2] = total[:, k * LANES : (k + 1) * LANES]
        turn = (((1,), (1,)), ((), ()))
        both = lax.dot_general(col_stack[0 : 2 * dim, cols], high, turn, preferred_element_type=F32)
        rest = lax.dot_general(col_stack[0:dim, cols], low, turn, preferred_element_type=F32)
        total = both[0:dim] + both[dim:] + rest
        for i in range(n_row):
            row_term[i] = row_term[i] + total[:, i * LANES : (i + 1) * LANES]
        return carry

    lax.fori_loop(0, n_chunks, grads, 0)


def grads(target, core, row_blocks, col_blocks, counts, masses):
    n_row, dim, _ = row_blocks.shape
    n_col = col_blocks.shape[0]
    deep = -(-3 * dim // 256) * 256
    tile_rows = n_row * LANES
    tile_cols = n_col * LANES
    return pl.pallas_call(
        grad_kernel,
        name="tile_grads",
        grid_spec=pltpu.PrefetchScalarGridSpec(
            num_scalar_prefetch=2,
            grid=(1,),
            in_specs=[pl.BlockSpec(memory_space=pltpu.VMEM)] * 4,
            out_specs=[pl.BlockSpec(memory_space=pltpu.VMEM)] * 2,
            scratch_shapes=[
                pltpu.VMEM((tile_rows, tile_cols), F32),
                pltpu.VMEM((deep, tile_cols), BF16),
                pltpu.VMEM((2 * dim, tile_rows), BF16),
                pltpu.VMEM((tile_rows, deep), BF16),
                pltpu.VMEM((tile_rows, LANES), F32),
                pltpu.VMEM((n_col, LANES), F32),
                pltpu.VMEM(counts.shape, F32),
            ],
        ),
        out_shape=[
            jax.ShapeDtypeStruct((n_row, dim, LANES), F32),
            jax.ShapeDtypeStruct((CORES, n_col // CORES, dim, LANES), F32),
        ],
        compiler_params=pltpu.CompilerParams(vmem_limit_bytes=60 << 20),
    )(target, core, row_blocks, col_blocks, counts, masses)


def swap_sum(value, axis, size, bit):
    return value + lax.ppermute(value, axis, [(i, i ^ bit) for i in range(size)])


def per_device(blocks, plan, live, row_emb, col_emb, row_acc, col_acc):
    n_z = lax.axis_size("col")
    n_row_axis = GRID_X * GRID_Y * CORES
    dim, words = row_emb.shape
    padded = -(-dim // 16) * 16
    pad = ((0, padded - dim), (0, 0))
    row_blocks = lax.all_gather(jnp.pad(row_emb, pad), "col", axis=0)
    col_blocks = lax.all_gather(jnp.pad(col_emb, pad), ROW, axis=0)
    sub_rows, sub_cols = blocks.shape[5:]
    slots_each = blocks.shape[4]
    arrived = lax.all_to_all(
        blocks.reshape(-1, slots_each, sub_rows, sub_cols), ALL, split_axis=0, concat_axis=0, tiled=True
    ).reshape(-1, sub_rows, sub_cols)
    places = plan[0, 0]
    alive = lax.broadcasted_iota(jnp.int32, places.shape, 2) < live[0, 0][:, :, None]
    target = jnp.where(alive, places, places[:, :, :1]).reshape(-1)
    tile_rows, tile_cols = words * n_z, words * n_row_axis
    counts, part = place(
        target, alive.astype(jnp.int32).reshape(-1), arrived, tile_rows // sub_rows, tile_cols // sub_cols
    )
    n_col, n_row = tile_cols // LANES, tile_rows // LANES
    row_part = part[n_col:]
    for bit in (1, 2, 4):
        row_part = swap_sum(row_part, "col", n_z, bit)
    col_part = jnp.concatenate([part[:n_col], row_part[n_row:]], axis=0)
    col_part = swap_sum(col_part, "core", CORES, 1)
    for axis, size in (("y", GRID_Y), ("x", GRID_X)):
        for bit in (1, 2):
            col_part = swap_sum(col_part, axis, size, bit)
    masses = jnp.concatenate([col_part[:n_col], row_part[:n_row], col_part[n_col:]], axis=0)
    core = lax.axis_index("core").astype(jnp.int32)
    row_term, col_term = grads(target, core.reshape(1), row_blocks, col_blocks, counts, masses)
    row_grad = lax.psum_scatter(row_term, "col", scatter_dimension=0, tiled=False)
    half = col_term[0] + lax.ppermute(col_term[1], "core", [(0, 1), (1, 0)])
    col_grad = jnp.sum(lax.all_to_all(half, ("x", "y"), split_axis=0, concat_axis=0, tiled=True), axis=0)
    loss_scale = 4.0 * float(words * n_z * n_row_axis) ** (-0.5)
    row_share = row_grad[:dim] * loss_scale
    col_share = col_grad[:dim] * loss_scale
    new_row_acc = row_acc + row_share * row_share
    new_col_acc = col_acc + col_share * col_share
    new_row_emb = row_emb - LEARNING_RATE * row_share / jnp.sqrt(new_row_acc)
    new_col_emb = col_emb - LEARNING_RATE * col_share / jnp.sqrt(new_col_acc)
    return (new_row_emb, new_col_emb, new_row_acc, new_col_acc)


def solution(mesh):
    n_z = mesh.devices.shape[1]
    inner = Mesh(mesh.devices.reshape(GRID_X, GRID_Y, CORES, n_z), ROW + ("col",))
    row_words = P(None, ROW + ("col",))
    col_words = P(None, ("col",) + ROW)
    return jax.shard_map(
        per_device,
        mesh=inner,
        in_specs=(P(ROW, "col"), P(ROW, "col"), P(ROW, "col"), row_words, col_words, row_words, col_words),
        out_specs=(row_words, col_words, row_words, col_words),
        check_vma=False,
    )
```

```python
import functools

import jax
import jax.numpy as jnp
from jax import lax
from jax.experimental import pallas as pl
from jax.experimental.pallas import tpu as pltpu
from jax.sharding import Mesh, PartitionSpec as P

LEARNING_RATE = 0.2
GRID_X, GRID_Y, CORES = 4, 4, 2
ROW = ("x", "y", "core")
ALL = ("col", "x", "y", "core")
LANES = 128
BLOCKS = 4
F32 = jnp.float32
BF16 = jnp.bfloat16


def split(value):
    high = value.astype(BF16)
    return high, (value - high.astype(F32)).astype(BF16)


def place_kernel(target, alive, arrived, counts_out, mass_out, dense, row_sums, col_sums):
    slots = arrived.shape[0]
    columns = col_sums.shape[0]
    shift = columns.bit_length() - 1
    row_words = row_sums.shape[0] // LANES * 8
    row_sums[...] = jnp.zeros(row_sums.shape, F32)
    col_sums[...] = jnp.zeros(col_sums.shape, F32)
    blank = jnp.zeros(arrived.shape[1:], F32)

    def clear(p, carry):
        dense[target[p]] = blank
        return carry

    lax.fori_loop(0, slots, clear, 0, unroll=8)

    def add(p, carry):
        place = target[p]
        value = jnp.where(alive[p] > 0, arrived[p], 0.0)
        row, column = lax.shift_right_logical(place, shift), place & (columns - 1)
        dense[place] = dense[place] + value
        row_sums[row] = row_sums[row] + value
        col_sums[column] = col_sums[column] + value
        return carry

    lax.fori_loop(0, slots, add, 0, unroll=8)

    def read(p, carry):
        counts_out[p] = dense[target[p]]
        return carry

    lax.fori_loop(0, slots, read, 0, unroll=8)
    col_part = jnp.sum(col_sums[...], axis=1)
    mass_out[0:columns, :] = col_part
    row_part = lax.dot_general(
        jnp.ones((8, LANES), F32),
        row_sums[...].reshape(-1, LANES),
        (((1,), (1,)), ((), ())),
        precision=lax.Precision.HIGHEST,
        preferred_element_type=F32,
    )
    for i in range(row_words):
        mass_out[columns + i : columns + i + 1, :] = row_part[0:1, i * LANES : (i + 1) * LANES]
    mass_out[columns + row_words :, :] = jnp.full((8, LANES), jnp.sum(col_part), F32)


def whole(count):
    return [pl.BlockSpec(memory_space=pltpu.VMEM)] * count


def place(target, alive, arrived, grid_rows, grid_columns):
    slots = arrived.shape[0]
    return pl.pallas_call(
        place_kernel,
        name="place_counts",
        grid_spec=pltpu.PrefetchScalarGridSpec(
            num_scalar_prefetch=2,
            grid=(1,),
            in_specs=whole(1),
            out_specs=whole(2),
            scratch_shapes=[
                pltpu.VMEM((grid_rows * grid_columns, 8, LANES), F32),
                pltpu.VMEM((grid_rows, 8, LANES), F32),
                pltpu.VMEM((grid_columns, 8, LANES), F32),
            ],
        ),
        out_shape=[
            jax.ShapeDtypeStruct((slots, 8, LANES), F32),
            jax.ShapeDtypeStruct((grid_columns + grid_rows * 8 // LANES + 8, LANES), F32),
        ],
        compiler_params=pltpu.CompilerParams(vmem_limit_bytes=22 << 20),
    )(target, alive, arrived)


def sort_kernel(target, order, offsets, cursor, *, columns):
    slots = target.shape[0]
    chunks = columns // BLOCKS
    mask = columns - 1
    low = BLOCKS.bit_length() - 1
    for k in range(chunks + 1):
        cursor[k] = 0

    def count(p, carry):
        k = lax.shift_right_logical(target[p] & mask, low)
        cursor[k] = cursor[k] + 1
        return carry

    lax.fori_loop(0, slots, count, 0, unroll=4)
    first = jnp.int32(0)
    for k in range(chunks):
        size = cursor[k]
        offsets[k] = first
        cursor[k] = first
        first = first + size
    offsets[chunks] = first

    def drop(p, carry):
        k = lax.shift_right_logical(target[p] & mask, low)
        at = cursor[k]
        order[at] = p
        cursor[k] = at + 1
        return carry

    lax.fori_loop(0, slots, drop, 0, unroll=4)


def sort_slots(target, columns):
    chunks = columns // BLOCKS
    smem = pl.BlockSpec(memory_space=pltpu.SMEM)
    return pl.pallas_call(
        functools.partial(sort_kernel, columns=columns),
        name="sort_slots",
        in_specs=[smem],
        out_specs=[smem, smem],
        out_shape=[
            jax.ShapeDtypeStruct(target.shape, jnp.int32),
            jax.ShapeDtypeStruct((chunks + 1,), jnp.int32),
        ],
        scratch_shapes=[pltpu.SMEM((chunks + 1,), jnp.int32)],
    )(target)


def taller(value, padded):
    return jnp.concatenate([value, jnp.zeros((padded - value.shape[0], LANES), F32)], axis=0)


def turn_kernel(row_blocks, row_stack, row_turned):
    padded = row_stack.shape[0] // 2
    deep = row_turned.shape[1]
    for i in range(row_blocks.shape[0]):
        high, low = split(taller(row_blocks[i], padded))
        here = slice(i * LANES, (i + 1) * LANES)
        row_stack[0:padded, here] = high
        row_stack[padded:, here] = low
        high32, low32 = high.astype(F32), low.astype(F32)
        tall = jnp.concatenate(
            [high32, high32, low32, jnp.zeros((deep - 3 * padded, LANES), F32)], axis=0
        )
        row_turned[here, :] = (0.5 * tall.T).astype(BF16)


def turn(row_blocks, padded, deep):
    words = row_blocks.shape[0] * LANES
    return pl.pallas_call(
        turn_kernel,
        name="turn_rows",
        in_specs=whole(1),
        out_specs=whole(2),
        out_shape=[
            jax.ShapeDtypeStruct((2 * padded, words), BF16),
            jax.ShapeDtypeStruct((words, deep), BF16),
        ],
        compiler_params=pltpu.CompilerParams(vmem_limit_bytes=24 << 20),
    )(row_blocks)


def score_kernel(row_turned, col_blocks, *rest):
    scores, col_stack, tall = rest[-3:]
    padded = col_stack.shape[0] // 2
    tall[3 * padded :, :] = jnp.zeros((tall.shape[0] - 3 * padded, tall.shape[1]), BF16)
    for k in range(BLOCKS):
        high, low = split(taller(col_blocks[k], padded))
        here = slice(k * LANES, (k + 1) * LANES)
        col_stack[0:padded, here] = high
        col_stack[padded:, here] = low
        tall[0:padded, here] = high
        tall[padded : 2 * padded, here] = low
        tall[2 * padded : 3 * padded, here] = high
    product = jnp.dot(row_turned[...], tall[...], preferred_element_type=F32)
    for k in range(BLOCKS):
        scores[:, k] = product[:, k * LANES : (k + 1) * LANES].reshape(-1, 8, LANES)


def score(row_turned, col_blocks, padded, first, count, earlier):
    words, deep = row_turned.shape
    n_col, dim, _ = col_blocks.shape
    width = BLOCKS * LANES
    ready = [] if earlier is None else list(earlier)
    return pl.pallas_call(
        score_kernel,
        name="score_piece",
        grid_spec=pltpu.PrefetchScalarGridSpec(
            num_scalar_prefetch=0,
            grid=(count,),
            in_specs=[
                pl.BlockSpec((words, deep), lambda g: (0, 0)),
                pl.BlockSpec((BLOCKS, dim, LANES), lambda g: (first + g, 0, 0)),
            ]
            + [pl.BlockSpec(memory_space=pltpu.HBM)] * len(ready),
            out_specs=[
                pl.BlockSpec((words // 8, BLOCKS, 8, LANES), lambda g: (0, first + g, 0, 0)),
                pl.BlockSpec((2 * padded, width), lambda g: (0, first + g)),
            ],
            scratch_shapes=[pltpu.VMEM((deep, width), BF16)],
        ),
        out_shape=[
            pltpu.HBM((words // 8, n_col, 8, LANES), F32),
            pltpu.HBM((2 * padded, n_col * LANES), BF16),
        ],
        input_output_aliases={2: 0, 3: 1} if ready else {},
        compiler_params=pltpu.CompilerParams(vmem_limit_bytes=24 << 20),
    )(row_turned, pltpu.with_memory_space_constraint(col_blocks, pltpu.HBM), *ready)


def grad_kernel(
    target, order, offsets, core, scores, counts, masses, row_stack,
    own, other, high_out, low_out,
    grads, row_bias, col_bias,
):
    ct = pl.program_id(0)
    n_col = col_bias.shape[0]
    n_row = row_stack.shape[1] // LANES
    padded = row_stack.shape[0] // 2
    shift = n_col.bit_length() - 1

    @pl.when(ct == 0)
    def _():
        log_total = jnp.log(masses[n_col + n_row : n_col + n_row + 1, :])
        col_bias[...] = 0.5 * (jnp.log(masses[0:n_col, :]) - log_total)
        row_logs = 0.5 * jnp.log(masses[n_col : n_col + n_row, :])
        for i in range(n_row):
            turned = jnp.broadcast_to(row_logs[i : i + 1, :], (LANES, LANES)).T
            row_bias[i * LANES // 8 : (i + 1) * LANES // 8] = turned.reshape(-1, 8, LANES)

    for k in range(BLOCKS):
        near = col_bias[pl.ds(ct * BLOCKS + k, 1), :]
        grads[:, k] = 0.5 * jnp.tanh(scores[:, k] + row_bias[...] + near) + 0.5
    begin = offsets[ct]
    end = offsets[ct + 1]

    def counted(step, carry):
        found = []
        for u in range(8):
            p = order[jnp.minimum(begin + step * 8 + u, end - 1)]
            place = target[p]
            row = lax.shift_right_logical(place, shift)
            column = place & (n_col - 1)
            k = column & (BLOCKS - 1)
            count = counts[p]
            score = scores[row, k] + row_bias[row] + col_bias[pl.ds(column, 1), :]
            fresh = (0.1 + 0.25 * jnp.sqrt(count)) * (2.0 * score - jnp.log(count))
            found.append((row, k, fresh))
        for row, k, fresh in found:
            grads[row, k] = fresh
        return carry

    lax.fori_loop(0, lax.shift_right_logical(end - begin + 7, 3), counted, 0)
    for k in range(BLOCKS):
        here = slice(k * LANES, (k + 1) * LANES)
        high, low = split(grads[:, k].reshape(-1, LANES))
        high_out[:, here] = high
        low_out[:, here] = low
    both = jnp.dot(row_stack[...], high_out[...], preferred_element_type=F32)
    rest = jnp.dot(row_stack[0:padded, :], low_out[...], preferred_element_type=F32)
    total = both[0:padded] + both[padded:] + rest
    parts = [total[:, k * LANES : (k + 1) * LANES] for k in range(BLOCKS)]
    mine = core[0] == 0
    for k in range(0, BLOCKS, 2):
        own[k // 2] = jnp.where(mine, parts[k], parts[k + 1])
        other[k // 2] = jnp.where(mine, parts[k + 1], parts[k])


def col_grads(target, order, offsets, core, scores, counts, masses, row_stack):
    grid_rows, n_col = scores.shape[:2]
    padded = row_stack.shape[0] // 2
    words = grid_rows * 8
    width = BLOCKS * LANES
    halves = BLOCKS // CORES
    term = jax.ShapeDtypeStruct((n_col // CORES, padded, LANES), F32)
    wide = pltpu.HBM((words, n_col * LANES), BF16)
    return pl.pallas_call(
        grad_kernel,
        name="col_grads",
        grid_spec=pltpu.PrefetchScalarGridSpec(
            num_scalar_prefetch=4,
            grid=(n_col // BLOCKS,),
            in_specs=[pl.BlockSpec((grid_rows, BLOCKS, 8, LANES), lambda g, *_: (0, g, 0, 0))] + whole(3),
            out_specs=[
                pl.BlockSpec((halves, padded, LANES), lambda g, *_: (g, 0, 0)),
                pl.BlockSpec((halves, padded, LANES), lambda g, *_: (g, 0, 0)),
                pl.BlockSpec((words, width), lambda g, *_: (0, g)),
                pl.BlockSpec((words, width), lambda g, *_: (0, g)),
            ],
            scratch_shapes=[
                pltpu.VMEM((grid_rows, BLOCKS, 8, LANES), F32),
                pltpu.VMEM((grid_rows, 8, LANES), F32),
                pltpu.VMEM((n_col, LANES), F32),
            ],
        ),
        out_shape=[term, term, wide, wide],
        compiler_params=pltpu.CompilerParams(vmem_limit_bytes=26 << 20),
    )(target, order, offsets, core, pltpu.with_memory_space_constraint(scores, pltpu.HBM), counts, masses, row_stack)


def row_kernel(col_stack, high, low, row_term):
    padded = col_stack.shape[0] // 2

    @pl.when(pl.program_id(0) == 0)
    def _():
        row_term[...] = jnp.zeros(row_term.shape, F32)

    turned = (((1,), (1,)), ((), ()))
    both = lax.dot_general(col_stack[...], high[...], turned, preferred_element_type=F32)
    rest = lax.dot_general(col_stack[0:padded, :], low[...], turned, preferred_element_type=F32)
    total = both[0:padded] + both[padded:] + rest
    for i in range(row_term.shape[0]):
        row_term[i] = row_term[i] + total[:, i * LANES : (i + 1) * LANES]


def row_grads(col_stack, high, low):
    words, n_words = high.shape
    width = BLOCKS * LANES
    padded = col_stack.shape[0] // 2
    return pl.pallas_call(
        row_kernel,
        name="row_grads",
        grid=(n_words // width,),
        in_specs=[
            pl.BlockSpec((2 * padded, width), lambda g: (0, g)),
            pl.BlockSpec((words, width), lambda g: (0, g)),
            pl.BlockSpec((words, width), lambda g: (0, g)),
        ],
        out_specs=pl.BlockSpec((words // LANES, padded, LANES), lambda g: (0, 0, 0)),
        out_shape=jax.ShapeDtypeStruct((words // LANES, padded, LANES), F32),
        compiler_params=pltpu.CompilerParams(vmem_limit_bytes=32 << 20),
    )(*(pltpu.with_memory_space_constraint(value, pltpu.HBM) for value in (col_stack, high, low)))


def swap_sum(value, axis, size, bit):
    return value + lax.ppermute(value, axis, [(i, i ^ bit) for i in range(size)])


def per_device(blocks, plan, live, row_emb, col_emb, row_acc, col_acc):
    n_z = lax.axis_size("col")
    n_row_axis = GRID_X * GRID_Y * CORES
    dim, words = row_emb.shape
    padded = -(-dim // 16) * 16
    deep = -(-3 * padded // 256) * 256
    col_blocks = lax.all_gather(col_emb, ROW, axis=0)
    row_emb_late, col_blocks = lax.optimization_barrier((row_emb, col_blocks))
    row_blocks = lax.all_gather(row_emb_late, "col", axis=0)
    sub_rows, sub_cols = blocks.shape[5:]
    slots_each = blocks.shape[4]
    arrived = lax.all_to_all(
        blocks.reshape(-1, slots_each, sub_rows, sub_cols), ALL, split_axis=0, concat_axis=0, tiled=True
    ).reshape(-1, sub_rows, sub_cols)
    places = plan[0, 0]
    alive = lax.broadcasted_iota(jnp.int32, places.shape, 2) < live[0, 0][:, :, None]
    target = jnp.where(alive, places, places[:, :, :1]).reshape(-1)
    tile_rows, tile_cols = words * n_z, words * n_row_axis
    n_col, n_row = tile_cols // LANES, tile_rows // LANES
    order, offsets = sort_slots(target, n_col)
    target, order, offsets = lax.optimization_barrier((target, order, offsets))
    counts, part = place(
        target, alive.astype(jnp.int32).reshape(-1), arrived, tile_rows // sub_rows, n_col
    )
    row_part = part[n_col:]
    for bit in (1, 2, 4):
        row_part = swap_sum(row_part, "col", n_z, bit)
    col_part = jnp.concatenate([part[:n_col], row_part[n_row:]], axis=0)
    col_part, row_blocks = lax.optimization_barrier((col_part, row_blocks))
    row_stack, row_turned = turn(row_blocks, padded, deep)
    col_part = swap_sum(col_part, "core", CORES, 1)
    scored = None
    first = 0
    chunks = n_col // BLOCKS
    for axis, bit in (("y", 1), ("y", 2), ("x", 1), ("x", 2)):
        col_part, row_turned = lax.optimization_barrier((col_part, row_turned))
        col_part = swap_sum(col_part, axis, GRID_X, bit)
        scored = score(row_turned, col_blocks, padded, first, chunks // 4, scored)
        col_part, scored = lax.optimization_barrier((col_part, scored))
        first += chunks // 4
    scores, col_stack = scored
    masses = jnp.concatenate([col_part[:n_col], row_part[:n_row], col_part[n_col:]], axis=0)
    core = lax.axis_index("core").astype(jnp.int32).reshape(1)
    own, other, high, low = col_grads(target, order, offsets, core, scores, counts, masses, row_stack)
    swapped = lax.ppermute(other, "core", [(0, 1), (1, 0)])
    row_term = row_grads(col_stack, high, low)
    row_grad = lax.psum_scatter(row_term, "col", scatter_dimension=0, tiled=False)
    half = own + swapped
    col_grad = jnp.sum(lax.all_to_all(half, ("x", "y"), split_axis=0, concat_axis=0, tiled=True), axis=0)
    loss_scale = 4.0 * float(words * n_z * n_row_axis) ** (-0.5)
    row_share = row_grad[:dim] * loss_scale
    col_share = col_grad[:dim] * loss_scale
    new_row_acc = row_acc + row_share * row_share
    new_col_acc = col_acc + col_share * col_share
    new_row_emb = row_emb - LEARNING_RATE * row_share / jnp.sqrt(new_row_acc)
    new_col_emb = col_emb - LEARNING_RATE * col_share / jnp.sqrt(new_col_acc)
    return (new_row_emb, new_col_emb, new_row_acc, new_col_acc)


def solution(mesh):
    n_z = mesh.devices.shape[1]
    inner = Mesh(mesh.devices.reshape(GRID_X, GRID_Y, CORES, n_z), ROW + ("col",))
    row_words = P(None, ROW + ("col",))
    col_words = P(None, ("col",) + ROW)
    return jax.shard_map(
        per_device,
        mesh=inner,
        in_specs=(P(ROW, "col"), P(ROW, "col"), P(ROW, "col"), row_words, col_words, row_words, col_words),
        out_specs=(row_words, col_words, row_words, col_words),
        check_vma=False,
    )
```

```python
import functools

import jax
import jax.numpy as jnp
from jax import lax
from jax.experimental import pallas as pl
from jax.experimental.pallas import tpu as pltpu
from jax.sharding import Mesh, PartitionSpec as P

LEARNING_RATE = 0.2
GRID_X, GRID_Y, CORES = 4, 4, 2
ROW = ("x", "y", "core")
ALL = ("col", "x", "y", "core")
LANES = 128
BLOCKS = 4
F32 = jnp.float32
BF16 = jnp.bfloat16


def split(value):
    high = value.astype(BF16)
    return high, (value - high.astype(F32)).astype(BF16)


def place_kernel(target, alive, arrived, counts_out, mass_out, dense, row_sums, col_sums):
    slots = arrived.shape[0]
    columns = col_sums.shape[0]
    shift = columns.bit_length() - 1
    row_words = row_sums.shape[0] // LANES * 8
    row_sums[...] = jnp.zeros(row_sums.shape, F32)
    col_sums[...] = jnp.zeros(col_sums.shape, F32)
    blank = jnp.zeros(arrived.shape[1:], F32)

    def clear(p, carry):
        dense[target[p]] = blank
        return carry

    lax.fori_loop(0, slots, clear, 0, unroll=8)

    def add(p, carry):
        place = target[p]
        value = jnp.where(alive[p] > 0, arrived[p], 0.0)
        row, column = lax.shift_right_logical(place, shift), place & (columns - 1)
        dense[place] = dense[place] + value
        row_sums[row] = row_sums[row] + value
        col_sums[column] = col_sums[column] + value
        return carry

    lax.fori_loop(0, slots, add, 0, unroll=8)

    def read(p, carry):
        counts_out[p] = dense[target[p]]
        return carry

    lax.fori_loop(0, slots, read, 0, unroll=8)
    col_part = jnp.sum(col_sums[...], axis=1)
    mass_out[0:columns, :] = col_part
    row_part = lax.dot_general(
        jnp.ones((8, LANES), F32),
        row_sums[...].reshape(-1, LANES),
        (((1,), (1,)), ((), ())),
        precision=lax.Precision.HIGHEST,
        preferred_element_type=F32,
    )
    for i in range(row_words):
        mass_out[columns + i : columns + i + 1, :] = row_part[0:1, i * LANES : (i + 1) * LANES]
    mass_out[columns + row_words :, :] = jnp.full((8, LANES), jnp.sum(col_part), F32)


def whole(count):
    return [pl.BlockSpec(memory_space=pltpu.VMEM)] * count


def place(target, alive, arrived, grid_rows, grid_columns):
    slots = arrived.shape[0]
    return pl.pallas_call(
        place_kernel,
        name="place_counts",
        grid_spec=pltpu.PrefetchScalarGridSpec(
            num_scalar_prefetch=2,
            grid=(1,),
            in_specs=whole(1),
            out_specs=whole(2),
            scratch_shapes=[
                pltpu.VMEM((grid_rows * grid_columns, 8, LANES), F32),
                pltpu.VMEM((grid_rows, 8, LANES), F32),
                pltpu.VMEM((grid_columns, 8, LANES), F32),
            ],
        ),
        out_shape=[
            jax.ShapeDtypeStruct((slots, 8, LANES), F32),
            jax.ShapeDtypeStruct((grid_columns + grid_rows * 8 // LANES + 8, LANES), F32),
        ],
        compiler_params=pltpu.CompilerParams(vmem_limit_bytes=22 << 20),
    )(target, alive, arrived)


def chunk_of(place, core, columns):
    column = place & (columns - 1)
    seat = lax.shift_right_logical(column, 1)
    far = (column & 1) ^ core
    chunk = (1 - far) * (columns // 2 // BLOCKS) + lax.shift_right_logical(seat, BLOCKS.bit_length() - 1)
    return chunk, seat & (BLOCKS - 1), column


def sort_kernel(target, core, order, offsets, cursor, *, columns):
    slots = target.shape[0]
    chunks = columns // BLOCKS
    for k in range(chunks + 1):
        cursor[k] = 0

    def count(p, carry):
        k = chunk_of(target[p], core[0], columns)[0]
        cursor[k] = cursor[k] + 1
        return carry

    lax.fori_loop(0, slots, count, 0, unroll=4)
    first = jnp.int32(0)
    for k in range(chunks):
        size = cursor[k]
        offsets[k] = first
        cursor[k] = first
        first = first + size
    offsets[chunks] = first

    def drop(p, carry):
        k = chunk_of(target[p], core[0], columns)[0]
        at = cursor[k]
        order[at] = p
        cursor[k] = at + 1
        return carry

    lax.fori_loop(0, slots, drop, 0, unroll=4)


def sort_slots(target, core, columns):
    chunks = columns // BLOCKS
    smem = pl.BlockSpec(memory_space=pltpu.SMEM)
    return pl.pallas_call(
        functools.partial(sort_kernel, columns=columns),
        name="sort_slots",
        in_specs=[smem, smem],
        out_specs=[smem, smem],
        out_shape=[
            jax.ShapeDtypeStruct(target.shape, jnp.int32),
            jax.ShapeDtypeStruct((chunks + 1,), jnp.int32),
        ],
        scratch_shapes=[pltpu.SMEM((chunks + 1,), jnp.int32)],
    )(target, core)


def taller(value, padded):
    return jnp.concatenate([value, jnp.zeros((padded - value.shape[0], LANES), F32)], axis=0)


def turn_kernel(row_blocks, row_stack, row_turned):
    padded = row_stack.shape[0] // 2
    deep = row_turned.shape[1]
    for i in range(row_blocks.shape[0]):
        high, low = split(taller(row_blocks[i], padded))
        here = slice(i * LANES, (i + 1) * LANES)
        row_stack[0:padded, here] = high
        row_stack[padded:, here] = low
        high32, low32 = high.astype(F32), low.astype(F32)
        tall = jnp.concatenate(
            [high32, high32, low32, jnp.zeros((deep - 3 * padded, LANES), F32)], axis=0
        )
        row_turned[here, :] = (0.5 * tall.T).astype(BF16)


def turn(row_blocks, padded, deep):
    words = row_blocks.shape[0] * LANES
    return pl.pallas_call(
        turn_kernel,
        name="turn_rows",
        in_specs=whole(1),
        out_specs=whole(2),
        out_shape=[
            jax.ShapeDtypeStruct((2 * padded, words), BF16),
            jax.ShapeDtypeStruct((words, deep), BF16),
        ],
        compiler_params=pltpu.CompilerParams(vmem_limit_bytes=24 << 20),
    )(row_blocks)


def stack_kernel(core, col_blocks, far, near):
    pairs = col_blocks.shape[0] // CORES
    deep = far.shape[0]
    dim = -(-col_blocks.shape[1] // 16) * 16
    mine = core[0] == 0
    for i in range(pairs):
        first, second = col_blocks[2 * i], col_blocks[2 * i + 1]
        here = slice(i * LANES, (i + 1) * LANES)
        for out, value in ((far, jnp.where(mine, second, first)), (near, jnp.where(mine, first, second))):
            high, low = split(taller(value, dim))
            out[0:dim, here] = high
            out[dim : 2 * dim, here] = low
            out[2 * dim : 3 * dim, here] = high
            out[3 * dim :, here] = jnp.zeros((deep - 3 * dim, LANES), BF16)


def stack_cols(core, col_blocks, deep):
    n_col, dim, _ = col_blocks.shape
    half = pltpu.HBM((deep, n_col // CORES * LANES), BF16)
    out = pl.BlockSpec((deep, BLOCKS * LANES), lambda g, *_: (0, g))
    return pl.pallas_call(
        stack_kernel,
        name="stack_columns",
        grid_spec=pltpu.PrefetchScalarGridSpec(
            num_scalar_prefetch=1,
            grid=(n_col // BLOCKS // CORES,),
            in_specs=[pl.BlockSpec((BLOCKS * CORES, dim, LANES), lambda g, *_: (g, 0, 0))],
            out_specs=[out, out],
        ),
        out_shape=[half, half],
        compiler_params=pltpu.CompilerParams(vmem_limit_bytes=14 << 20),
    )(core, pltpu.with_memory_space_constraint(col_blocks, pltpu.HBM))


def part_kernel(
    target, order, offsets, core, row_turned, row_stack, col_stack, counts, masses, *rest, near
):
    col_term, row_term, scores, grads, row_bias, col_bias = rest[-6:]
    padded, n_row = row_term.shape[1], row_term.shape[0]
    n_col = col_bias.shape[0]
    ct = pl.program_id(0)
    chunks = pl.num_programs(0)
    shift = n_col.bit_length() - 1
    side = core[0] if near else 1 - core[0]

    @pl.when(ct == 0)
    def _():
        log_total = jnp.log(masses[n_col + n_row : n_col + n_row + 1, :])
        col_bias[...] = 0.5 * (jnp.log(masses[0:n_col, :]) - log_total)
        row_logs = 0.5 * jnp.log(masses[n_col : n_col + n_row, :])
        for i in range(n_row):
            turned = jnp.broadcast_to(row_logs[i : i + 1, :], (LANES, LANES)).T
            row_bias[i * LANES // 8 : (i + 1) * LANES // 8] = turned.reshape(-1, 8, LANES)
        row_term[...] = rest[0][...] if near else jnp.zeros(row_term.shape, F32)

    product = jnp.dot(row_turned[...], col_stack[...], preferred_element_type=F32)
    for k in range(BLOCKS):
        bias = col_bias[pl.ds((ct * BLOCKS + k) * 2 + side, 1), :]
        value = product[:, k * LANES : (k + 1) * LANES].reshape(-1, 8, LANES) + row_bias[...] + bias
        scores[:, k] = value
        grads[:, k] = 0.5 * jnp.tanh(value) + 0.5
    at = ct + (chunks if near else 0)
    begin = offsets[at]
    end = offsets[at + 1]

    def counted(step, carry):
        found = []
        for u in range(8):
            p = order[jnp.minimum(begin + step * 8 + u, end - 1)]
            place = target[p]
            row = lax.shift_right_logical(place, shift)
            k = lax.shift_right_logical(place & (n_col - 1), 1) & (BLOCKS - 1)
            count = counts[p]
            fresh = (0.1 + 0.25 * jnp.sqrt(count)) * (2.0 * scores[row, k] - jnp.log(count))
            found.append((row, k, fresh))
        for row, k, fresh in found:
            grads[row, k] = fresh
        return carry

    lax.fori_loop(0, lax.shift_right_logical(end - begin + 7, 3), counted, 0)
    pieces = [split(grads[:, k].reshape(-1, LANES)) for k in range(BLOCKS)]
    high = jnp.concatenate([piece[0] for piece in pieces], axis=1)
    low = jnp.concatenate([piece[1] for piece in pieces], axis=1)
    both = jnp.dot(row_stack[...], high, preferred_element_type=F32)
    rest_ = jnp.dot(row_stack[0:padded, :], low, preferred_element_type=F32)
    total = both[0:padded] + both[padded:] + rest_
    for k in range(BLOCKS):
        col_term[k] = total[:, k * LANES : (k + 1) * LANES]
    turned = (((1,), (1,)), ((), ()))
    both = lax.dot_general(col_stack[0 : 2 * padded, :], high, turned, preferred_element_type=F32)
    rest_ = lax.dot_general(col_stack[0:padded, :], low, turned, preferred_element_type=F32)
    total = both[0:padded] + both[padded:] + rest_
    for i in range(n_row):
        row_term[i] = row_term[i] + total[:, i * LANES : (i + 1) * LANES]


def part_grads(scalars, row_turned, row_stack, col_stack, counts, masses, earlier):
    words, deep = row_turned.shape
    padded = row_stack.shape[0] // 2
    blocks = col_stack.shape[1] // LANES
    near = earlier is not None
    ready = [earlier] if near else []
    return pl.pallas_call(
        functools.partial(part_kernel, near=near),
        name="near_grads" if near else "far_grads",
        grid_spec=pltpu.PrefetchScalarGridSpec(
            num_scalar_prefetch=4,
            grid=(blocks // BLOCKS,),
            in_specs=whole(2)
            + [pl.BlockSpec((deep, BLOCKS * LANES), lambda g, *_: (0, g))]
            + whole(2 + len(ready)),
            out_specs=[pl.BlockSpec((BLOCKS, padded, LANES), lambda g, *_: (g, 0, 0))] + whole(1),
            scratch_shapes=[
                pltpu.VMEM((words // 8, BLOCKS, 8, LANES), F32),
                pltpu.VMEM((words // 8, BLOCKS, 8, LANES), F32),
                pltpu.VMEM((words // 8, 8, LANES), F32),
                pltpu.VMEM((blocks * CORES, LANES), F32),
            ],
        ),
        out_shape=[
            jax.ShapeDtypeStruct((blocks, padded, LANES), F32),
            jax.ShapeDtypeStruct((words // LANES, padded, LANES), F32),
        ],
        compiler_params=pltpu.CompilerParams(vmem_limit_bytes=36 << 20),
    )(*scalars, row_turned, row_stack, pltpu.with_memory_space_constraint(col_stack, pltpu.HBM), counts, masses, *ready)


def swap_sum(value, axis, size, bit):
    return value + lax.ppermute(value, axis, [(i, i ^ bit) for i in range(size)])


def per_device(blocks, plan, live, row_emb, col_emb, row_acc, col_acc):
    n_z = lax.axis_size("col")
    n_row_axis = GRID_X * GRID_Y * CORES
    dim, words = row_emb.shape
    padded = -(-dim // 16) * 16
    deep = -(-3 * padded // 256) * 256
    core = lax.axis_index("core").astype(jnp.int32).reshape(1)
    places = plan[0, 0]
    alive = lax.broadcasted_iota(jnp.int32, places.shape, 2) < live[0, 0][:, :, None]
    target = jnp.where(alive, places, places[:, :, :1]).reshape(-1)
    tile_rows, tile_cols = words * n_z, words * n_row_axis
    n_col, n_row = tile_cols // LANES, tile_rows // LANES
    order, offsets = sort_slots(target, core, n_col)
    col_blocks = lax.all_gather(col_emb, ROW, axis=0)
    row_emb_late, col_blocks, order, offsets = lax.optimization_barrier((row_emb, col_blocks, order, offsets))
    row_blocks = lax.all_gather(row_emb_late, "col", axis=0)
    sub_rows, sub_cols = blocks.shape[5:]
    slots_each = blocks.shape[4]
    arrived = lax.all_to_all(
        blocks.reshape(-1, slots_each, sub_rows, sub_cols), ALL, split_axis=0, concat_axis=0, tiled=True
    ).reshape(-1, sub_rows, sub_cols)
    counts, part = place(
        target, alive.astype(jnp.int32).reshape(-1), arrived, tile_rows // sub_rows, n_col
    )
    row_part = part[n_col:]
    row_part = swap_sum(row_part, "col", n_z, 1)
    row_part = swap_sum(row_part, "col", n_z, 2)
    row_part, core = lax.optimization_barrier((row_part, core))
    far_stack, near_stack = stack_cols(core, col_blocks, deep)
    row_part = swap_sum(row_part, "col", n_z, 4)
    row_part, far_stack, near_stack = lax.optimization_barrier((row_part, far_stack, near_stack))
    col_part = jnp.concatenate([part[:n_col], row_part[n_row:]], axis=0)
    col_part = swap_sum(col_part, "core", CORES, 1)
    for axis, bit in (("y", 1), ("y", 2), ("x", 1)):
        col_part = swap_sum(col_part, axis, GRID_X, bit)
    col_part, row_blocks = lax.optimization_barrier((col_part, row_blocks))
    row_stack, row_turned = turn(row_blocks, padded, deep)
    col_part = swap_sum(col_part, "x", GRID_X, 2)
    masses = jnp.concatenate([col_part[:n_col], row_part[:n_row], col_part[n_col:]], axis=0)
    scalars = (target, order, offsets, core)
    far_term, row_term = part_grads(scalars, row_turned, row_stack, far_stack, counts, masses, None)
    swapped = lax.ppermute(far_term, "core", [(0, 1), (1, 0)])
    near_term, row_term = part_grads(scalars, row_turned, row_stack, near_stack, counts, masses, row_term)
    row_grad = lax.psum_scatter(row_term, "col", scatter_dimension=0, tiled=False)
    half = near_term + swapped
    col_grad = jnp.sum(lax.all_to_all(half, ("x", "y"), split_axis=0, concat_axis=0, tiled=True), axis=0)
    loss_scale = 4.0 * float(words * n_z * n_row_axis) ** (-0.5)
    row_share = row_grad[:dim] * loss_scale
    col_share = col_grad[:dim] * loss_scale
    new_row_acc = row_acc + row_share * row_share
    new_col_acc = col_acc + col_share * col_share
    new_row_emb = row_emb - LEARNING_RATE * row_share / jnp.sqrt(new_row_acc)
    new_col_emb = col_emb - LEARNING_RATE * col_share / jnp.sqrt(new_col_acc)
    return (new_row_emb, new_col_emb, new_row_acc, new_col_acc)


def solution(mesh):
    n_z = mesh.devices.shape[1]
    inner = Mesh(mesh.devices.reshape(GRID_X, GRID_Y, CORES, n_z), ROW + ("col",))
    row_words = P(None, ROW + ("col",))
    col_words = P(None, ("col",) + ROW)
    return jax.shard_map(
        per_device,
        mesh=inner,
        in_specs=(P(ROW, "col"), P(ROW, "col"), P(ROW, "col"), row_words, col_words, row_words, col_words),
        out_specs=(row_words, col_words, row_words, col_words),
        check_vma=False,
    )
```

```python
import functools

import jax
import jax.numpy as jnp
from jax import lax
from jax.experimental import pallas as pl
from jax.experimental.pallas import tpu as pltpu
from jax.sharding import Mesh, PartitionSpec as P

LEARNING_RATE = 0.2
GRID_X, GRID_Y, CORES = 4, 4, 2
ROW = ("x", "y", "core")
ALL = ("col", "x", "y", "core")
LANES = 128
BLOCKS = 4
F32 = jnp.float32
BF16 = jnp.bfloat16


def split(value):
    high = value.astype(BF16)
    return high, (value - high.astype(F32)).astype(BF16)


def place_kernel(target, alive, arrived, counts_out, mass_out, dense, row_sums, col_sums):
    slots = arrived.shape[0]
    columns = col_sums.shape[0]
    shift = columns.bit_length() - 1
    row_words = row_sums.shape[0] // LANES * 8
    row_sums[...] = jnp.zeros(row_sums.shape, F32)
    col_sums[...] = jnp.zeros(col_sums.shape, F32)
    blank = jnp.zeros(arrived.shape[1:], F32)

    def clear(p, carry):
        dense[target[p]] = blank
        return carry

    lax.fori_loop(0, slots, clear, 0, unroll=8)

    def add(p, carry):
        place = target[p]
        value = jnp.where(alive[p] > 0, arrived[p], 0.0)
        row, column = lax.shift_right_logical(place, shift), place & (columns - 1)
        dense[place] = dense[place] + value
        row_sums[row] = row_sums[row] + value
        col_sums[column] = col_sums[column] + value
        return carry

    lax.fori_loop(0, slots, add, 0, unroll=8)

    def read(p, carry):
        counts_out[p] = dense[target[p]]
        return carry

    lax.fori_loop(0, slots, read, 0, unroll=8)
    col_part = jnp.sum(col_sums[...], axis=1)
    mass_out[0:columns, :] = col_part
    row_part = lax.dot_general(
        jnp.ones((8, LANES), F32),
        row_sums[...].reshape(-1, LANES),
        (((1,), (1,)), ((), ())),
        precision=lax.Precision.HIGHEST,
        preferred_element_type=F32,
    )
    for i in range(row_words):
        mass_out[columns + i : columns + i + 1, :] = row_part[0:1, i * LANES : (i + 1) * LANES]
    mass_out[columns + row_words :, :] = jnp.full((8, LANES), jnp.sum(col_part), F32)


def whole(count):
    return [pl.BlockSpec(memory_space=pltpu.VMEM)] * count


def place(target, alive, arrived, grid_rows, grid_columns):
    slots = arrived.shape[0]
    return pl.pallas_call(
        place_kernel,
        name="place_counts",
        grid_spec=pltpu.PrefetchScalarGridSpec(
            num_scalar_prefetch=2,
            grid=(1,),
            in_specs=whole(1),
            out_specs=whole(2),
            scratch_shapes=[
                pltpu.VMEM((grid_rows * grid_columns, 8, LANES), F32),
                pltpu.VMEM((grid_rows, 8, LANES), F32),
                pltpu.VMEM((grid_columns, 8, LANES), F32),
            ],
        ),
        out_shape=[
            jax.ShapeDtypeStruct((slots, 8, LANES), F32),
            jax.ShapeDtypeStruct((grid_columns + grid_rows * 8 // LANES + 8, LANES), F32),
        ],
        compiler_params=pltpu.CompilerParams(vmem_limit_bytes=22 << 20),
    )(target, alive, arrived)


def chunk_of(place, core, columns):
    column = place & (columns - 1)
    seat = lax.shift_right_logical(column, 1)
    far = (column & 1) ^ core
    chunk = (1 - far) * (columns // 2 // BLOCKS) + lax.shift_right_logical(seat, BLOCKS.bit_length() - 1)
    return chunk, seat & (BLOCKS - 1)


def sort_kernel(target, core, order, spots, offsets, cursor, *, columns):
    slots = target.shape[0]
    chunks = columns // BLOCKS
    for k in range(chunks + 1):
        cursor[k] = 0

    def count(p, carry):
        k = chunk_of(target[p], core[0], columns)[0]
        cursor[k] = cursor[k] + 1
        return carry

    lax.fori_loop(0, slots, count, 0, unroll=4)
    first = jnp.int32(0)
    for k in range(chunks):
        size = cursor[k]
        offsets[k] = first
        cursor[k] = first
        first = first + size
    offsets[chunks] = first

    def drop(p, carry):
        place = target[p]
        k, seat = chunk_of(place, core[0], columns)
        at = cursor[k]
        order[at] = p
        spots[at] = lax.shift_right_logical(place, columns.bit_length() - 1) * BLOCKS + seat
        cursor[k] = at + 1
        return carry

    lax.fori_loop(0, slots, drop, 0, unroll=4)


def sort_slots(target, core, columns):
    chunks = columns // BLOCKS
    smem = pl.BlockSpec(memory_space=pltpu.SMEM)
    return pl.pallas_call(
        functools.partial(sort_kernel, columns=columns),
        name="sort_slots",
        in_specs=[smem, smem],
        out_specs=[smem] * 3,
        out_shape=[
            jax.ShapeDtypeStruct(target.shape, jnp.int32),
            jax.ShapeDtypeStruct(target.shape, jnp.int32),
            jax.ShapeDtypeStruct((chunks + 1,), jnp.int32),
        ],
        scratch_shapes=[pltpu.SMEM((chunks + 1,), jnp.int32)],
    )(target, core)


def taller(value, padded):
    return jnp.concatenate([value, jnp.zeros((padded - value.shape[0], LANES), F32)], axis=0)


def turn_kernel(row_blocks, row_stack, row_turned):
    padded = row_stack.shape[0] // 2
    deep = row_turned.shape[1]
    for i in range(row_blocks.shape[0]):
        high, low = split(taller(row_blocks[i], padded))
        here = slice(i * LANES, (i + 1) * LANES)
        row_stack[0:padded, here] = high
        row_stack[padded:, here] = low
        high32, low32 = high.astype(F32), low.astype(F32)
        tall = jnp.concatenate(
            [high32, high32, low32, jnp.zeros((deep - 3 * padded, LANES), F32)], axis=0
        )
        row_turned[here, :] = (0.5 * tall.T).astype(BF16)


def turn(row_blocks, padded, deep):
    words = row_blocks.shape[0] * LANES
    return pl.pallas_call(
        turn_kernel,
        name="turn_rows",
        in_specs=whole(1),
        out_specs=whole(2),
        out_shape=[
            jax.ShapeDtypeStruct((2 * padded, words), BF16),
            jax.ShapeDtypeStruct((words, deep), BF16),
        ],
        compiler_params=pltpu.CompilerParams(vmem_limit_bytes=24 << 20),
    )(row_blocks)


def stack_kernel(core, col_blocks, out):
    deep = out.shape[0]
    dim = -(-col_blocks.shape[2] // 16) * 16
    for i in range(BLOCKS):
        high, low = split(taller(col_blocks[i, 0], dim))
        here = slice(i * LANES, (i + 1) * LANES)
        out[0:dim, here] = high
        out[dim : 2 * dim, here] = low
        out[2 * dim : 3 * dim, here] = high
        out[3 * dim :, here] = jnp.zeros((deep - 3 * dim, LANES), BF16)


def stack_cols(core, col_blocks, deep, near):
    n_col, dim, _ = col_blocks.shape
    seats = n_col // CORES
    col_blocks = pltpu.with_memory_space_constraint(col_blocks.reshape(seats, CORES, dim, LANES), pltpu.HBM)
    pick = lambda g, core: (g, core[0] if near else 1 - core[0], 0, 0)
    return pl.pallas_call(
        stack_kernel,
        name="stack_near" if near else "stack_far",
        grid_spec=pltpu.PrefetchScalarGridSpec(
            num_scalar_prefetch=1,
            grid=(seats // BLOCKS,),
            in_specs=[pl.BlockSpec((BLOCKS, 1, dim, LANES), pick)],
            out_specs=pl.BlockSpec((deep, BLOCKS * LANES), lambda g, *_: (0, g)),
        ),
        out_shape=pltpu.HBM((deep, seats * LANES), BF16),
        compiler_params=pltpu.CompilerParams(vmem_limit_bytes=14 << 20),
    )(core, col_blocks)


def part_kernel(
    order, spots, offsets, core, row_turned, row_stack, col_stack, counts_far, masses, *rest, near
):
    col_term, row_term, scores, grads, row_bias, col_bias, counts, arrival = rest[-8:]
    padded, n_row = row_term.shape[1], row_term.shape[0]
    n_col = col_bias.shape[0]
    ct = pl.program_id(0)
    chunks = pl.num_programs(0)
    side = core[0] if near else 1 - core[0]

    fetch = pltpu.make_async_copy(counts_far, counts, arrival)

    @pl.when(ct == 0)
    def _():
        fetch.start()
        log_total = jnp.log(masses[n_col + n_row : n_col + n_row + 1, :])
        col_bias[...] = 0.5 * (jnp.log(masses[0:n_col, :]) - log_total)
        row_logs = 0.5 * jnp.log(masses[n_col : n_col + n_row, :])
        for i in range(n_row):
            turned = jnp.broadcast_to(row_logs[i : i + 1, :], (LANES, LANES)).T
            row_bias[i * LANES // 8 : (i + 1) * LANES // 8] = turned.reshape(-1, 8, LANES)
        row_term[...] = rest[0][...] if near else jnp.zeros(row_term.shape, F32)

    product = jnp.dot(row_turned[...], col_stack[...], preferred_element_type=F32)
    for k in range(BLOCKS):
        bias = col_bias[pl.ds((ct * BLOCKS + k) * 2 + side, 1), :]
        value = product[:, k * LANES : (k + 1) * LANES].reshape(-1, 8, LANES) + row_bias[...] + bias
        scores[:, k] = value
        grads[:, k] = 0.5 * jnp.tanh(value) + 0.5
    here = ct + (chunks if near else 0)
    begin = offsets[here]
    end = offsets[here + 1]

    @pl.when(ct == 0)
    def _():
        fetch.wait()

    def counted(step, carry):
        found = []
        for u in range(8):
            at = jnp.minimum(begin + step * 8 + u, end - 1)
            spot = spots[at]
            row, k = lax.shift_right_logical(spot, BLOCKS.bit_length() - 1), spot & (BLOCKS - 1)
            count = counts[order[at]]
            fresh = (0.1 + 0.25 * jnp.sqrt(count)) * (2.0 * scores[row, k] - jnp.log(count))
            found.append((row, k, fresh))
        for row, k, fresh in found:
            grads[row, k] = fresh
        return carry

    lax.fori_loop(0, lax.shift_right_logical(end - begin + 7, 3), counted, 0)
    pieces = [split(grads[:, k].reshape(-1, LANES)) for k in range(BLOCKS)]
    high = jnp.concatenate([piece[0] for piece in pieces], axis=1)
    low = jnp.concatenate([piece[1] for piece in pieces], axis=1)
    both = jnp.dot(row_stack[...], high, preferred_element_type=F32)
    rest_ = jnp.dot(row_stack[0:padded, :], low, preferred_element_type=F32)
    total = both[0:padded] + both[padded:] + rest_
    for k in range(BLOCKS):
        col_term[k] = total[:, k * LANES : (k + 1) * LANES]
    turned = (((1,), (1,)), ((), ()))
    both = lax.dot_general(col_stack[0 : 2 * padded, :], high, turned, preferred_element_type=F32)
    rest_ = lax.dot_general(col_stack[0:padded, :], low, turned, preferred_element_type=F32)
    total = both[0:padded] + both[padded:] + rest_
    for i in range(n_row):
        row_term[i] = row_term[i] + total[:, i * LANES : (i + 1) * LANES]


def part_grads(scalars, row_turned, row_stack, col_stack, counts, masses, earlier):
    words, deep = row_turned.shape
    padded = row_stack.shape[0] // 2
    blocks = col_stack.shape[1] // LANES
    near = earlier is not None
    ready = [earlier] if near else []
    return pl.pallas_call(
        functools.partial(part_kernel, near=near),
        name="near_grads" if near else "far_grads",
        grid_spec=pltpu.PrefetchScalarGridSpec(
            num_scalar_prefetch=4,
            grid=(blocks // BLOCKS,),
            in_specs=whole(2)
            + [pl.BlockSpec((deep, BLOCKS * LANES), lambda g, *_: (0, g))]
            + [pl.BlockSpec(memory_space=pltpu.HBM)]
            + whole(1 + len(ready)),
            out_specs=[pl.BlockSpec((BLOCKS, padded, LANES), lambda g, *_: (g, 0, 0)), pl.BlockSpec((words // LANES, padded, LANES), lambda g, *_: (0, 0, 0))],
            scratch_shapes=[
                pltpu.VMEM((words // 8, BLOCKS, 8, LANES), F32),
                pltpu.VMEM((words // 8, BLOCKS, 8, LANES), F32),
                pltpu.VMEM((words // 8, 8, LANES), F32),
                pltpu.VMEM((blocks * CORES, LANES), F32),
                pltpu.VMEM(counts.shape, F32),
                pltpu.SemaphoreType.DMA(()),
            ],
        ),
        out_shape=[
            jax.ShapeDtypeStruct((blocks, padded, LANES), F32),
            (pltpu.HBM if near else jax.ShapeDtypeStruct)((words // LANES, padded, LANES), F32),
        ],
        compiler_params=pltpu.CompilerParams(vmem_limit_bytes=36 << 20),
    )(*scalars, row_turned, row_stack, pltpu.with_memory_space_constraint(col_stack, pltpu.HBM), pltpu.with_memory_space_constraint(counts, pltpu.HBM), masses, *ready)


def swap_sum(value, axis, size, bit):
    return value + lax.ppermute(value, axis, [(i, i ^ bit) for i in range(size)])


def per_device(blocks, plan, live, row_emb, col_emb, row_acc, col_acc):
    n_z = lax.axis_size("col")
    n_row_axis = GRID_X * GRID_Y * CORES
    dim, words = row_emb.shape
    padded = -(-dim // 16) * 16
    deep = -(-3 * padded // 256) * 256
    core = lax.axis_index("core").astype(jnp.int32).reshape(1)
    places = plan[0, 0]
    alive = lax.broadcasted_iota(jnp.int32, places.shape, 2) < live[0, 0][:, :, None]
    target = jnp.where(alive, places, places[:, :, :1]).reshape(-1)
    tile_rows, tile_cols = words * n_z, words * n_row_axis
    n_col, n_row = tile_cols // LANES, tile_rows // LANES
    order, spots, offsets = sort_slots(target, core, n_col)
    col_blocks = lax.all_gather(col_emb, ROW, axis=0)
    row_emb_late, col_blocks, order, spots, offsets = lax.optimization_barrier(
        (row_emb, col_blocks, order, spots, offsets)
    )
    row_blocks = lax.all_gather(row_emb_late, "col", axis=0)
    sub_rows, sub_cols = blocks.shape[5:]
    slots_each = blocks.shape[4]
    arrived = lax.all_to_all(
        blocks.reshape(-1, slots_each, sub_rows, sub_cols), ALL, split_axis=0, concat_axis=0, tiled=True
    ).reshape(-1, sub_rows, sub_cols)
    counts, part = place(
        target, alive.astype(jnp.int32).reshape(-1), arrived, tile_rows // sub_rows, n_col
    )
    row_part = part[n_col:]
    row_part = swap_sum(row_part, "col", n_z, 1)
    row_part = swap_sum(row_part, "col", n_z, 2)
    row_part = swap_sum(row_part, "col", n_z, 4)
    col_part = jnp.concatenate([part[:n_col], row_part[n_row:]], axis=0)
    col_part = swap_sum(col_part, "core", CORES, 1)
    col_part, col_blocks = lax.optimization_barrier((col_part, col_blocks))
    col_part = swap_sum(col_part, "y", GRID_Y, 1)
    far_stack = stack_cols(core, col_blocks, deep, False)
    col_part, far_stack, col_blocks = lax.optimization_barrier((col_part, far_stack, col_blocks))
    col_part = swap_sum(col_part, "y", GRID_Y, 2)
    near_stack = stack_cols(core, col_blocks, deep, True)
    col_part, near_stack = lax.optimization_barrier((col_part, near_stack))
    col_part = swap_sum(col_part, "x", GRID_X, 1)
    col_part, row_blocks = lax.optimization_barrier((col_part, row_blocks))
    row_stack, row_turned = turn(row_blocks, padded, deep)
    col_part = swap_sum(col_part, "x", GRID_X, 2)
    masses = jnp.concatenate([col_part[:n_col], row_part[:n_row], col_part[n_col:]], axis=0)
    scalars = (order, spots, offsets, core)
    far_term, row_term = part_grads(scalars, row_turned, row_stack, far_stack, counts, masses, None)
    swapped = lax.ppermute(far_term, "core", [(0, 1), (1, 0)])
    near_term, row_term = part_grads(scalars, row_turned, row_stack, near_stack, counts, masses, row_term)
    row_grad = lax.psum_scatter(row_term, "col", scatter_dimension=0, tiled=False)
    half = near_term + swapped
    col_grad = jnp.sum(lax.all_to_all(half, ("x", "y"), split_axis=0, concat_axis=0, tiled=True), axis=0)
    loss_scale = 4.0 * float(words * n_z * n_row_axis) ** (-0.5)
    row_share = row_grad[:dim] * loss_scale
    col_share = col_grad[:dim] * loss_scale
    new_row_acc = row_acc + row_share * row_share
    new_col_acc = col_acc + col_share * col_share
    new_row_emb = row_emb - LEARNING_RATE * row_share / jnp.sqrt(new_row_acc)
    new_col_emb = col_emb - LEARNING_RATE * col_share / jnp.sqrt(new_col_acc)
    return (new_row_emb, new_col_emb, new_row_acc, new_col_acc)


def solution(mesh):
    n_z = mesh.devices.shape[1]
    inner = Mesh(mesh.devices.reshape(GRID_X, GRID_Y, CORES, n_z), ROW + ("col",))
    row_words = P(None, ROW + ("col",))
    col_words = P(None, ("col",) + ROW)
    return jax.shard_map(
        per_device,
        mesh=inner,
        in_specs=(P(ROW, "col"), P(ROW, "col"), P(ROW, "col"), row_words, col_words, row_words, col_words),
        out_specs=(row_words, col_words, row_words, col_words),
        check_vma=False,
    )
```

```python
import functools

import jax
import jax.numpy as jnp
from jax import lax
from jax.experimental import pallas as pl
from jax.experimental.pallas import tpu as pltpu
from jax.sharding import Mesh, PartitionSpec as P

LEARNING_RATE = 0.2
GRID_X, GRID_Y, CORES = 4, 4, 2
ROW = ("x", "y", "core")
ALL = ("col", "x", "y", "core")
LANES = 128
BLOCKS = 8
F32 = jnp.float32
BF16 = jnp.bfloat16


def split(value):
    high = value.astype(BF16)
    return high, (value - high.astype(F32)).astype(BF16)


def place_kernel(target, alive, arrived, counts_out, mass_out, dense, row_sums, col_sums):
    slots = arrived.shape[0]
    columns = col_sums.shape[0]
    shift = columns.bit_length() - 1
    row_words = row_sums.shape[0] // LANES * 8
    row_sums[...] = jnp.zeros(row_sums.shape, F32)
    col_sums[...] = jnp.zeros(col_sums.shape, F32)
    blank = jnp.zeros(arrived.shape[1:], F32)

    def clear(p, carry):
        dense[target[p]] = blank
        return carry

    lax.fori_loop(0, slots, clear, 0, unroll=8)

    def add(p, carry):
        place = target[p]
        value = jnp.where(alive[p] > 0, arrived[p], 0.0)
        row, column = lax.shift_right_logical(place, shift), place & (columns - 1)
        dense[place] = dense[place] + value
        row_sums[row] = row_sums[row] + value
        col_sums[column] = col_sums[column] + value
        return carry

    lax.fori_loop(0, slots, add, 0, unroll=8)

    def read(p, carry):
        counts_out[p] = dense[target[p]]
        return carry

    lax.fori_loop(0, slots, read, 0, unroll=8)
    col_part = jnp.sum(col_sums[...], axis=1)
    mass_out[0:columns, :] = col_part
    row_part = lax.dot_general(
        jnp.ones((8, LANES), F32),
        row_sums[...].reshape(-1, LANES),
        (((1,), (1,)), ((), ())),
        precision=lax.Precision.HIGHEST,
        preferred_element_type=F32,
    )
    for i in range(row_words):
        mass_out[columns + i : columns + i + 1, :] = row_part[0:1, i * LANES : (i + 1) * LANES]
    mass_out[columns + row_words :, :] = jnp.full((8, LANES), jnp.sum(col_part), F32)


def whole(count):
    return [pl.BlockSpec(memory_space=pltpu.VMEM)] * count


def place(target, alive, arrived, grid_rows, grid_columns):
    slots = arrived.shape[0]
    return pl.pallas_call(
        place_kernel,
        name="place_counts",
        grid_spec=pltpu.PrefetchScalarGridSpec(
            num_scalar_prefetch=2,
            grid=(1,),
            in_specs=whole(1),
            out_specs=whole(2),
            scratch_shapes=[
                pltpu.VMEM((grid_rows * grid_columns, 8, LANES), F32),
                pltpu.VMEM((grid_rows, 8, LANES), F32),
                pltpu.VMEM((grid_columns, 8, LANES), F32),
            ],
        ),
        out_shape=[
            jax.ShapeDtypeStruct((slots, 8, LANES), F32),
            jax.ShapeDtypeStruct((grid_columns + grid_rows * 8 // LANES + 8, LANES), F32),
        ],
        compiler_params=pltpu.CompilerParams(vmem_limit_bytes=22 << 20),
    )(target, alive, arrived)


def chunk_of(place, core, columns):
    column = place & (columns - 1)
    seat = lax.shift_right_logical(column, 1)
    far = (column & 1) ^ core
    chunk = (1 - far) * (columns // 2 // BLOCKS) + lax.shift_right_logical(seat, BLOCKS.bit_length() - 1)
    return chunk, seat & (BLOCKS - 1)


def sort_kernel(target, core, order, spots, offsets, cursor, *, columns):
    slots = target.shape[0]
    chunks = columns // BLOCKS
    for k in range(chunks + 1):
        cursor[k] = 0

    def count(p, carry):
        k = chunk_of(target[p], core[0], columns)[0]
        cursor[k] = cursor[k] + 1
        return carry

    lax.fori_loop(0, slots, count, 0, unroll=4)
    first = jnp.int32(0)
    for k in range(chunks):
        size = cursor[k]
        offsets[k] = first
        cursor[k] = first
        first = first + size
    offsets[chunks] = first

    def drop(p, carry):
        place = target[p]
        k, seat = chunk_of(place, core[0], columns)
        at = cursor[k]
        order[at] = p
        spots[at] = lax.shift_right_logical(place, columns.bit_length() - 1) * BLOCKS + seat
        cursor[k] = at + 1
        return carry

    lax.fori_loop(0, slots, drop, 0, unroll=4)


def sort_slots(target, core, columns):
    chunks = columns // BLOCKS
    smem = pl.BlockSpec(memory_space=pltpu.SMEM)
    return pl.pallas_call(
        functools.partial(sort_kernel, columns=columns),
        name="sort_slots",
        in_specs=[smem, smem],
        out_specs=[smem] * 3,
        out_shape=[
            jax.ShapeDtypeStruct(target.shape, jnp.int32),
            jax.ShapeDtypeStruct(target.shape, jnp.int32),
            jax.ShapeDtypeStruct((chunks + 1,), jnp.int32),
        ],
        scratch_shapes=[pltpu.SMEM((chunks + 1,), jnp.int32)],
    )(target, core)


def taller(value, padded):
    return jnp.concatenate([value, jnp.zeros((padded - value.shape[0], LANES), F32)], axis=0)


def turn_kernel(row_blocks, row_stack, row_turned):
    padded = row_stack.shape[0] // 2
    deep = row_turned.shape[1]
    for i in range(row_blocks.shape[0]):
        high, low = split(taller(row_blocks[i], padded))
        here = slice(i * LANES, (i + 1) * LANES)
        row_stack[0:padded, here] = high
        row_stack[padded:, here] = low
        high32, low32 = high.astype(F32), low.astype(F32)
        tall = jnp.concatenate(
            [high32, high32, low32, jnp.zeros((deep - 3 * padded, LANES), F32)], axis=0
        )
        row_turned[here, :] = (0.5 * tall.T).astype(BF16)


def turn(row_blocks, padded, deep):
    words = row_blocks.shape[0] * LANES
    return pl.pallas_call(
        turn_kernel,
        name="turn_rows",
        in_specs=whole(1),
        out_specs=whole(2),
        out_shape=[
            jax.ShapeDtypeStruct((2 * padded, words), BF16),
            jax.ShapeDtypeStruct((words, deep), BF16),
        ],
        compiler_params=pltpu.CompilerParams(vmem_limit_bytes=24 << 20),
    )(row_blocks)


def stack_kernel(core, col_blocks, *rest):
    out = rest[-1]
    deep = out.shape[0]
    dim = -(-col_blocks.shape[2] // 16) * 16
    for i in range(col_blocks.shape[0]):
        high, low = split(taller(col_blocks[i, 0], dim))
        here = slice(i * LANES, (i + 1) * LANES)
        out[0:dim, here] = high
        out[dim : 2 * dim, here] = low
        out[2 * dim : 3 * dim, here] = high
        out[3 * dim :, here] = jnp.zeros((deep - 3 * dim, LANES), BF16)


def stack_cols(core, col_blocks, deep, near, earlier=None):
    n_col, dim, _ = col_blocks.shape
    seats = n_col // CORES
    step = BLOCKS // 2
    first = 0 if earlier is None else seats // step // 2
    ready = [] if earlier is None else [earlier]
    col_blocks = pltpu.with_memory_space_constraint(col_blocks.reshape(seats, CORES, dim, LANES), pltpu.HBM)
    pick = lambda g, core: (first + g, core[0] if near else 1 - core[0], 0, 0)
    return pl.pallas_call(
        stack_kernel,
        name="stack_near" if near else "stack_far",
        grid_spec=pltpu.PrefetchScalarGridSpec(
            num_scalar_prefetch=1,
            grid=(seats // step // 2,),
            in_specs=[pl.BlockSpec((step, 1, dim, LANES), pick)]
            + [pl.BlockSpec(memory_space=pltpu.HBM)] * len(ready),
            out_specs=pl.BlockSpec((deep, step * LANES), lambda g, *_: (0, first + g)),
        ),
        out_shape=pltpu.HBM((deep, seats * LANES), BF16),
        input_output_aliases={2: 0} if ready else {},
        compiler_params=pltpu.CompilerParams(vmem_limit_bytes=14 << 20),
    )(core, col_blocks, *ready)


def part_kernel(
    order, spots, offsets, core, row_turned, row_stack, col_stack, counts_far, masses, *rest, near
):
    col_term, row_term, scores, grads, row_bias, col_bias, counts, arrival = rest[-8:]
    padded, n_row = row_term.shape[1], row_term.shape[0]
    n_col = col_bias.shape[0]
    ct = pl.program_id(0)
    chunks = pl.num_programs(0)
    side = core[0] if near else 1 - core[0]

    fetch = pltpu.make_async_copy(counts_far, counts, arrival)

    @pl.when(ct == 0)
    def _():
        fetch.start()
        log_total = jnp.log(masses[n_col + n_row : n_col + n_row + 1, :])
        col_bias[...] = 0.5 * (jnp.log(masses[0:n_col, :]) - log_total)
        row_logs = 0.5 * jnp.log(masses[n_col : n_col + n_row, :])
        for i in range(n_row):
            turned = jnp.broadcast_to(row_logs[i : i + 1, :], (LANES, LANES)).T
            row_bias[i * LANES // 8 : (i + 1) * LANES // 8] = turned.reshape(-1, 8, LANES)
        row_term[...] = rest[0][...] if near else jnp.zeros(row_term.shape, F32)

    product = jnp.dot(row_turned[...], col_stack[...], preferred_element_type=F32)
    for k in range(BLOCKS):
        bias = col_bias[pl.ds((ct * BLOCKS + k) * 2 + side, 1), :]
        value = product[:, k * LANES : (k + 1) * LANES].reshape(-1, 8, LANES) + row_bias[...] + bias
        scores[:, k] = value
        grads[:, k] = 0.5 * jnp.tanh(value) + 0.5
    here = ct + (chunks if near else 0)
    begin = offsets[here]
    end = offsets[here + 1]

    @pl.when(ct == 0)
    def _():
        fetch.wait()

    def counted(step, carry):
        found = []
        for u in range(8):
            at = jnp.minimum(begin + step * 8 + u, end - 1)
            spot = spots[at]
            row, k = lax.shift_right_logical(spot, BLOCKS.bit_length() - 1), spot & (BLOCKS - 1)
            count = counts[order[at]]
            fresh = (0.1 + 0.25 * jnp.sqrt(count)) * (2.0 * scores[row, k] - jnp.log(count))
            found.append((row, k, fresh))
        for row, k, fresh in found:
            grads[row, k] = fresh
        return carry

    lax.fori_loop(0, lax.shift_right_logical(end - begin + 7, 3), counted, 0)
    pieces = [split(grads[:, k].reshape(-1, LANES)) for k in range(BLOCKS)]
    high = jnp.concatenate([piece[0] for piece in pieces], axis=1)
    low = jnp.concatenate([piece[1] for piece in pieces], axis=1)
    both = jnp.dot(row_stack[...], high, preferred_element_type=F32)
    rest_ = jnp.dot(row_stack[0:padded, :], low, preferred_element_type=F32)
    total = both[0:padded] + both[padded:] + rest_
    for k in range(BLOCKS):
        col_term[k] = total[:, k * LANES : (k + 1) * LANES]
    turned = (((1,), (1,)), ((), ()))
    both = lax.dot_general(col_stack[0 : 2 * padded, :], high, turned, preferred_element_type=F32)
    rest_ = lax.dot_general(col_stack[0:padded, :], low, turned, preferred_element_type=F32)
    total = both[0:padded] + both[padded:] + rest_
    for i in range(n_row):
        row_term[i] = row_term[i] + total[:, i * LANES : (i + 1) * LANES]


def part_grads(scalars, row_turned, row_stack, col_stack, counts, masses, earlier):
    words, deep = row_turned.shape
    padded = row_stack.shape[0] // 2
    blocks = col_stack.shape[1] // LANES
    near = earlier is not None
    ready = [earlier] if near else []
    return pl.pallas_call(
        functools.partial(part_kernel, near=near),
        name="near_grads" if near else "far_grads",
        grid_spec=pltpu.PrefetchScalarGridSpec(
            num_scalar_prefetch=4,
            grid=(blocks // BLOCKS,),
            in_specs=whole(2)
            + [pl.BlockSpec((deep, BLOCKS * LANES), lambda g, *_: (0, g))]
            + [pl.BlockSpec(memory_space=pltpu.HBM)]
            + whole(1 + len(ready)),
            out_specs=[pl.BlockSpec((BLOCKS, padded, LANES), lambda g, *_: (g, 0, 0)), pl.BlockSpec((words // LANES, padded, LANES), lambda g, *_: (0, 0, 0))],
            scratch_shapes=[
                pltpu.VMEM((words // 8, BLOCKS, 8, LANES), F32),
                pltpu.VMEM((words // 8, BLOCKS, 8, LANES), F32),
                pltpu.VMEM((words // 8, 8, LANES), F32),
                pltpu.VMEM((blocks * CORES, LANES), F32),
                pltpu.VMEM(counts.shape, F32),
                pltpu.SemaphoreType.DMA(()),
            ],
        ),
        out_shape=[
            jax.ShapeDtypeStruct((blocks, padded, LANES), F32),
            (pltpu.HBM if near else jax.ShapeDtypeStruct)((words // LANES, padded, LANES), F32),
        ],
        compiler_params=pltpu.CompilerParams(vmem_limit_bytes=36 << 20),
    )(*scalars, row_turned, row_stack, pltpu.with_memory_space_constraint(col_stack, pltpu.HBM), pltpu.with_memory_space_constraint(counts, pltpu.HBM), masses, *ready)


def swap_sum(value, axis, size, bit):
    return value + lax.ppermute(value, axis, [(i, i ^ bit) for i in range(size)])


def per_device(blocks, plan, live, row_emb, col_emb, row_acc, col_acc):
    n_z = lax.axis_size("col")
    n_row_axis = GRID_X * GRID_Y * CORES
    dim, words = row_emb.shape
    padded = -(-dim // 16) * 16
    deep = -(-3 * padded // 256) * 256
    core = lax.axis_index("core").astype(jnp.int32).reshape(1)
    places = plan[0, 0]
    alive = lax.broadcasted_iota(jnp.int32, places.shape, 2) < live[0, 0][:, :, None]
    target = jnp.where(alive, places, places[:, :, :1]).reshape(-1)
    tile_rows, tile_cols = words * n_z, words * n_row_axis
    n_col, n_row = tile_cols // LANES, tile_rows // LANES
    order, spots, offsets = sort_slots(target, core, n_col)
    col_blocks = lax.all_gather(col_emb, ROW, axis=0)
    row_emb_late, col_blocks, order, spots, offsets = lax.optimization_barrier(
        (row_emb, col_blocks, order, spots, offsets)
    )
    row_blocks = lax.all_gather(row_emb_late, "col", axis=0)
    sub_rows, sub_cols = blocks.shape[5:]
    slots_each = blocks.shape[4]
    arrived = lax.all_to_all(
        blocks.reshape(-1, slots_each, sub_rows, sub_cols), ALL, split_axis=0, concat_axis=0, tiled=True
    ).reshape(-1, sub_rows, sub_cols)
    counts, part = place(
        pltpu.with_memory_space_constraint(target, pltpu.HBM), alive.astype(jnp.int32).reshape(-1), arrived, tile_rows // sub_rows, n_col
    )
    row_part = part[n_col:]
    row_part = swap_sum(row_part, "col", n_z, 1)
    row_part = swap_sum(row_part, "col", n_z, 2)
    row_part, col_blocks = lax.optimization_barrier((row_part, col_blocks))
    row_part = swap_sum(row_part, "col", n_z, 4)
    far_stack = stack_cols(core, col_blocks, deep, False)
    row_part, far_stack = lax.optimization_barrier((row_part, far_stack))
    col_part = jnp.concatenate([part[:n_col], row_part[n_row:]], axis=0)
    col_part = swap_sum(col_part, "core", CORES, 1)
    col_part, far_stack, col_blocks = lax.optimization_barrier((col_part, far_stack, col_blocks))
    col_part = swap_sum(col_part, "y", GRID_Y, 1)
    far_stack = stack_cols(core, col_blocks, deep, False, far_stack)
    col_part, far_stack, col_blocks = lax.optimization_barrier((col_part, far_stack, col_blocks))
    col_part = swap_sum(col_part, "y", GRID_Y, 2)
    near_stack = stack_cols(core, col_blocks, deep, True)
    col_part, near_stack, col_blocks = lax.optimization_barrier((col_part, near_stack, col_blocks))
    col_part = swap_sum(col_part, "x", GRID_X, 1)
    near_stack = stack_cols(core, col_blocks, deep, True, near_stack)
    col_part, near_stack = lax.optimization_barrier((col_part, near_stack))
    col_part, row_blocks = lax.optimization_barrier((col_part, row_blocks))
    row_stack, row_turned = turn(row_blocks, padded, deep)
    col_part = swap_sum(col_part, "x", GRID_X, 2)
    masses = jnp.concatenate([col_part[:n_col], row_part[:n_row], col_part[n_col:]], axis=0)
    scalars = (order, spots, offsets, core)
    far_term, row_term = part_grads(scalars, row_turned, row_stack, far_stack, counts, masses, None)
    swapped = lax.ppermute(far_term, "core", [(0, 1), (1, 0)])
    near_term, row_term = part_grads(scalars, row_turned, row_stack, near_stack, counts, masses, row_term)
    row_grad = lax.psum_scatter(row_term, "col", scatter_dimension=0, tiled=False)
    half = near_term + swapped
    col_grad = jnp.sum(lax.all_to_all(half, ("x", "y"), split_axis=0, concat_axis=0, tiled=True), axis=0)
    loss_scale = 4.0 * float(words * n_z * n_row_axis) ** (-0.5)
    row_share = row_grad[:dim] * loss_scale
    col_share = col_grad[:dim] * loss_scale
    new_row_acc = row_acc + row_share * row_share
    new_col_acc = col_acc + col_share * col_share
    new_row_emb = row_emb - LEARNING_RATE * row_share / jnp.sqrt(new_row_acc)
    new_col_emb = col_emb - LEARNING_RATE * col_share / jnp.sqrt(new_col_acc)
    return (new_row_emb, new_col_emb, new_row_acc, new_col_acc)


def solution(mesh):
    n_z = mesh.devices.shape[1]
    inner = Mesh(mesh.devices.reshape(GRID_X, GRID_Y, CORES, n_z), ROW + ("col",))
    row_words = P(None, ROW + ("col",))
    col_words = P(None, ("col",) + ROW)
    return jax.shard_map(
        per_device,
        mesh=inner,
        in_specs=(P(ROW, "col"), P(ROW, "col"), P(ROW, "col"), row_words, col_words, row_words, col_words),
        out_specs=(row_words, col_words, row_words, col_words),
        check_vma=False,
    )
```

```python
import functools

import jax
import jax.numpy as jnp
from jax import lax
from jax.experimental import pallas as pl
from jax.experimental.pallas import tpu as pltpu
from jax.sharding import Mesh, PartitionSpec as P

LEARNING_RATE = 0.2
GRID_X, GRID_Y, CORES = 4, 4, 2
ROW = ("x", "y", "core")
ALL = ("col", "x", "y", "core")
LANES = 128
BLOCKS = 8
F32 = jnp.float32
BF16 = jnp.bfloat16


def split(value):
    high = value.astype(BF16)
    return high, (value - high.astype(F32)).astype(BF16)


def place_kernel(target, alive, arrived, counts_out, mass_out, dense, row_sums, col_sums):
    slots = arrived.shape[0]
    columns = col_sums.shape[0]
    shift = columns.bit_length() - 1
    row_words = row_sums.shape[0] // LANES * 8
    row_sums[...] = jnp.zeros(row_sums.shape, F32)
    col_sums[...] = jnp.zeros(col_sums.shape, F32)
    blank = jnp.zeros(arrived.shape[1:], F32)

    def clear(p, carry):
        dense[target[p]] = blank
        return carry

    lax.fori_loop(0, slots, clear, 0, unroll=8)

    def add(p, carry):
        place = target[p]
        value = jnp.where(alive[p] > 0, arrived[p], 0.0)
        row, column = lax.shift_right_logical(place, shift), place & (columns - 1)
        dense[place] = dense[place] + value
        row_sums[row] = row_sums[row] + value
        col_sums[column] = col_sums[column] + value
        return carry

    lax.fori_loop(0, slots, add, 0, unroll=8)

    def read(p, carry):
        counts_out[p] = dense[target[p]]
        return carry

    lax.fori_loop(0, slots, read, 0, unroll=8)
    col_part = jnp.sum(col_sums[...], axis=1)
    mass_out[0:columns, :] = col_part
    row_part = lax.dot_general(
        jnp.ones((8, LANES), F32),
        row_sums[...].reshape(-1, LANES),
        (((1,), (1,)), ((), ())),
        precision=lax.Precision.HIGHEST,
        preferred_element_type=F32,
    )
    for i in range(row_words):
        mass_out[columns + i : columns + i + 1, :] = row_part[0:1, i * LANES : (i + 1) * LANES]
    mass_out[columns + row_words :, :] = jnp.full((8, LANES), jnp.sum(col_part), F32)


def whole(count):
    return [pl.BlockSpec(memory_space=pltpu.VMEM)] * count


def place(target, alive, arrived, grid_rows, grid_columns):
    slots = arrived.shape[0]
    return pl.pallas_call(
        place_kernel,
        name="place_counts",
        grid_spec=pltpu.PrefetchScalarGridSpec(
            num_scalar_prefetch=2,
            grid=(1,),
            in_specs=whole(1),
            out_specs=whole(2),
            scratch_shapes=[
                pltpu.VMEM((grid_rows * grid_columns, 8, LANES), F32),
                pltpu.VMEM((grid_rows, 8, LANES), F32),
                pltpu.VMEM((grid_columns, 8, LANES), F32),
            ],
        ),
        out_shape=[
            jax.ShapeDtypeStruct((slots, 8, LANES), F32),
            jax.ShapeDtypeStruct((grid_columns + grid_rows * 8 // LANES + 8, LANES), F32),
        ],
        compiler_params=pltpu.CompilerParams(vmem_limit_bytes=22 << 20),
    )(target, alive, arrived)


def chunk_of(place, core, columns):
    column = place & (columns - 1)
    seat = lax.shift_right_logical(column, 1)
    far = (column & 1) ^ core
    chunk = (1 - far) * (columns // 2 // BLOCKS) + lax.shift_right_logical(seat, BLOCKS.bit_length() - 1)
    return chunk, seat & (BLOCKS - 1)


def sort_kernel(target, core, order, spots, offsets, cursor, *, columns):
    slots = target.shape[0]
    chunks = columns // BLOCKS
    for k in range(chunks + 1):
        cursor[k] = 0

    def count(p, carry):
        k = chunk_of(target[p], core[0], columns)[0]
        cursor[k] = cursor[k] + 1
        return carry

    lax.fori_loop(0, slots, count, 0, unroll=4)
    first = jnp.int32(0)
    for k in range(chunks):
        size = cursor[k]
        offsets[k] = first
        cursor[k] = first
        first = first + size
    offsets[chunks] = first

    def drop(p, carry):
        place = target[p]
        k, seat = chunk_of(place, core[0], columns)
        at = cursor[k]
        order[at] = p
        spots[at] = lax.shift_right_logical(place, columns.bit_length() - 1) * BLOCKS + seat
        cursor[k] = at + 1
        return carry

    lax.fori_loop(0, slots, drop, 0, unroll=4)


def sort_slots(target, core, columns):
    chunks = columns // BLOCKS
    smem = pl.BlockSpec(memory_space=pltpu.SMEM)
    return pl.pallas_call(
        functools.partial(sort_kernel, columns=columns),
        name="sort_slots",
        in_specs=[smem, smem],
        out_specs=[smem] * 3,
        out_shape=[
            jax.ShapeDtypeStruct(target.shape, jnp.int32),
            jax.ShapeDtypeStruct(target.shape, jnp.int32),
            jax.ShapeDtypeStruct((chunks + 1,), jnp.int32),
        ],
        scratch_shapes=[pltpu.SMEM((chunks + 1,), jnp.int32)],
    )(target, core)


def taller(value, padded):
    return jnp.concatenate([value, jnp.zeros((padded - value.shape[0], LANES), F32)], axis=0)


def turn_kernel(row_blocks, row_stack, row_turned):
    padded = row_stack.shape[0] // 2
    deep = row_turned.shape[1]
    for i in range(row_blocks.shape[0]):
        high, low = split(taller(row_blocks[i], padded))
        here = slice(i * LANES, (i + 1) * LANES)
        row_stack[0:padded, here] = high
        row_stack[padded:, here] = low
        high32, low32 = high.astype(F32), low.astype(F32)
        tall = jnp.concatenate(
            [high32, high32, low32, jnp.zeros((deep - 3 * padded, LANES), F32)], axis=0
        )
        row_turned[here, :] = (0.5 * tall.T).astype(BF16)


def turn(row_blocks, padded, deep):
    words = row_blocks.shape[0] * LANES
    return pl.pallas_call(
        turn_kernel,
        name="turn_rows",
        in_specs=whole(1),
        out_specs=whole(2),
        out_shape=[
            jax.ShapeDtypeStruct((2 * padded, words), BF16),
            jax.ShapeDtypeStruct((words, deep), BF16),
        ],
        compiler_params=pltpu.CompilerParams(vmem_limit_bytes=24 << 20),
    )(row_blocks)


def stack_kernel(core, col_blocks, *rest):
    out = rest[-1]
    dim = out.shape[0] // 2
    for i in range(col_blocks.shape[0]):
        high, low = split(taller(col_blocks[i, 0], dim))
        here = slice(i * LANES, (i + 1) * LANES)
        out[0:dim, here] = high
        out[dim:, here] = low


def stack_cols(core, col_blocks, padded, near, earlier=None):
    n_col, dim, _ = col_blocks.shape
    seats = n_col // CORES
    step = BLOCKS // 2
    first = 0 if earlier is None else seats // step // 2
    ready = [] if earlier is None else [earlier]
    col_blocks = pltpu.with_memory_space_constraint(col_blocks.reshape(seats, CORES, dim, LANES), pltpu.HBM)
    pick = lambda g, core: (first + g, core[0] if near else 1 - core[0], 0, 0)
    return pl.pallas_call(
        stack_kernel,
        name="stack_near" if near else "stack_far",
        grid_spec=pltpu.PrefetchScalarGridSpec(
            num_scalar_prefetch=1,
            grid=(seats // step // 2,),
            in_specs=[pl.BlockSpec((step, 1, dim, LANES), pick)]
            + [pl.BlockSpec(memory_space=pltpu.HBM)] * len(ready),
            out_specs=pl.BlockSpec((2 * padded, step * LANES), lambda g, *_: (0, first + g)),
        ),
        out_shape=pltpu.HBM((2 * padded, seats * LANES), BF16),
        input_output_aliases={2: 0} if ready else {},
        compiler_params=pltpu.CompilerParams(vmem_limit_bytes=14 << 20),
    )(core, col_blocks, *ready)


def part_kernel(
    order, spots, offsets, core, row_turned, row_stack, stack_far, counts_far, masses, *rest, near, first, merge
):
    merging = []
    if merge:
        *merging, rest = rest[1], rest[2], *rest[-2:], rest[:1] + rest[3:-2]
    col_term, row_term, scores, grads, row_bias, col_bias, counts, stacks = rest[-10:-2]
    arrival, stack_arrivals = rest[-2:]
    padded, n_row = row_term.shape[1], row_term.shape[0]
    n_col = col_bias.shape[0]
    step = pl.program_id(0)
    ct = step + first
    half_chunks = n_col // CORES // BLOCKS
    side = core[0] if near else 1 - core[0]

    width = BLOCKS * LANES
    fetch = pltpu.make_async_copy(counts_far, counts, arrival)

    def bring(chunk):
        cols = pl.ds(pl.multiple_of((first + chunk) * width, width), width)
        kept = stacks.at[chunk, pl.ds(0, 2 * padded), :]
        return pltpu.make_async_copy(stack_far.at[:, cols], kept, stack_arrivals.at[chunk])

    @pl.when(step == 0)
    def _():
        bring(0).start()
        fetch.start()
        for chunk in range(1, stacks.shape[0]):
            bring(chunk).start()
        log_total = jnp.log(masses[n_col + n_row : n_col + n_row + 1, :])
        col_bias[...] = 0.5 * (jnp.log(masses[0:n_col, :]) - log_total)
        row_logs = 0.5 * jnp.log(masses[n_col : n_col + n_row, :])
        for i in range(n_row):
            turned = jnp.broadcast_to(row_logs[i : i + 1, :], (LANES, LANES)).T
            row_bias[i * LANES // 8 : (i + 1) * LANES // 8] = turned.reshape(-1, 8, LANES)
        row_term[...] = rest[0][...] if near else jnp.zeros(row_term.shape, F32)

    bring(step).wait()
    stacks[step, 2 * padded : 3 * padded, :] = stacks[step, 0:padded, :]
    stacks[step, 3 * padded :, :] = jnp.zeros((stacks.shape[1] - 3 * padded, width), BF16)
    product = jnp.dot(row_turned[...], stacks[step], preferred_element_type=F32)
    for k in range(BLOCKS):
        bias = col_bias[pl.ds((ct * BLOCKS + k) * 2 + side, 1), :]
        value = product[:, k * LANES : (k + 1) * LANES].reshape(-1, 8, LANES) + row_bias[...] + bias
        scores[:, k] = value
        grads[:, k] = 0.5 * jnp.tanh(value) + 0.5
    here = ct + (half_chunks if near else 0)
    begin = offsets[here]
    end = offsets[here + 1]

    @pl.when(step == 0)
    def _():
        fetch.wait()

    def counted(group, carry):
        found = []
        for u in range(8):
            at = jnp.minimum(begin + group * 8 + u, end - 1)
            spot = spots[at]
            row, k = lax.shift_right_logical(spot, BLOCKS.bit_length() - 1), spot & (BLOCKS - 1)
            count = counts[order[at]]
            fresh = (0.1 + 0.25 * jnp.sqrt(count)) * (2.0 * scores[row, k] - jnp.log(count))
            found.append((row, k, fresh))
        for row, k, fresh in found:
            grads[row, k] = fresh
        return carry

    lax.fori_loop(0, lax.shift_right_logical(end - begin + 7, 3), counted, 0)
    if merge:
        piece, swapped, merged, leaves = merging
        merged[0 : first * BLOCKS] = swapped[0 : first * BLOCKS] + piece[...]
        parts = [pl.ds(0, first * BLOCKS), pl.ds(first * BLOCKS, BLOCKS)]
        leave = [
            pltpu.make_async_copy(merged.at[part], col_term.at[part], leaves.at[i])
            for i, part in enumerate(parts)
        ]
        leave[0].start()
    pieces = [split(grads[:, k].reshape(-1, LANES)) for k in range(BLOCKS)]
    high = jnp.concatenate([piece[0] for piece in pieces], axis=1)
    low = jnp.concatenate([piece[1] for piece in pieces], axis=1)
    both = jnp.dot(row_stack[...], high, preferred_element_type=F32)
    rest_ = jnp.dot(row_stack[0:padded, :], low, preferred_element_type=F32)
    total = both[0:padded] + both[padded:] + rest_
    for k in range(BLOCKS):
        block = total[:, k * LANES : (k + 1) * LANES]
        if merge:
            merged[first * BLOCKS + k] = swapped[first * BLOCKS + k] + block
        else:
            col_term[k] = block
    if merge:
        leave[1].start()
    turned = (((1,), (1,)), ((), ()))
    both = lax.dot_general(stacks[step, 0 : 2 * padded, :], high, turned, preferred_element_type=F32)
    rest_ = lax.dot_general(stacks[step, 0:padded, :], low, turned, preferred_element_type=F32)
    total = both[0:padded] + both[padded:] + rest_
    for i in range(n_row):
        row_term[i] = row_term[i] + total[:, i * LANES : (i + 1) * LANES]
    if merge:
        for copy in leave:
            copy.wait()


def part_grads(scalars, row_turned, row_stack, col_stack, counts, masses, earlier, first, count, extra=()):
    words, deep = row_turned.shape
    padded = row_stack.shape[0] // 2
    blocks = col_stack.shape[1] // LANES
    near = earlier is not None
    merge = bool(extra)
    ready = [earlier] if near else []
    out_blocks = blocks if merge else count * BLOCKS
    scratch = [
        pltpu.VMEM((blocks, padded, LANES), F32),
        pltpu.SemaphoreType.DMA((2,)),
    ]
    return pl.pallas_call(
        functools.partial(part_kernel, near=near, first=first, merge=merge),
        name="merge_grads" if merge else "near_grads" if near else "far_grads",
        grid_spec=pltpu.PrefetchScalarGridSpec(
            num_scalar_prefetch=4,
            grid=(count,),
            in_specs=whole(2)
            + [pl.BlockSpec(memory_space=pltpu.HBM)] * 2
            + whole(1 + len(ready) + len(extra)),
            out_specs=[
                pl.BlockSpec(memory_space=pltpu.HBM)
                if merge
                else pl.BlockSpec((BLOCKS, padded, LANES), lambda g, *_: (g, 0, 0)),
                pl.BlockSpec((words // LANES, padded, LANES), lambda g, *_: (0, 0, 0)),
            ],
            scratch_shapes=[
                pltpu.VMEM((words // 8, BLOCKS, 8, LANES), F32),
                pltpu.VMEM((words // 8, BLOCKS, 8, LANES), F32),
                pltpu.VMEM((words // 8, 8, LANES), F32),
                pltpu.VMEM((blocks * CORES, LANES), F32),
                pltpu.VMEM(counts.shape, F32),
                pltpu.VMEM((count, deep, BLOCKS * LANES), BF16),
                pltpu.SemaphoreType.DMA(()),
                pltpu.SemaphoreType.DMA((count,)),
            ]
            + (scratch if merge else []),
        ),
        out_shape=[
            (pltpu.HBM if merge else jax.ShapeDtypeStruct)((out_blocks, padded, LANES), F32),
            (pltpu.HBM if merge else jax.ShapeDtypeStruct)((words // LANES, padded, LANES), F32),
        ],
        compiler_params=pltpu.CompilerParams(vmem_limit_bytes=40 << 20),
    )(*scalars, row_turned, row_stack, pltpu.with_memory_space_constraint(col_stack, pltpu.HBM), pltpu.with_memory_space_constraint(counts, pltpu.HBM), masses, *ready, *extra)


def swap_sum(value, axis, size, bit):
    return value + lax.ppermute(value, axis, [(i, i ^ bit) for i in range(size)])


def per_device(blocks, plan, live, row_emb, col_emb, row_acc, col_acc):
    n_z = lax.axis_size("col")
    n_row_axis = GRID_X * GRID_Y * CORES
    dim, words = row_emb.shape
    padded = -(-dim // 16) * 16
    deep = -(-3 * padded // 256) * 256
    core = lax.axis_index("core").astype(jnp.int32).reshape(1)
    places = plan[0, 0]
    alive = lax.broadcasted_iota(jnp.int32, places.shape, 2) < live[0, 0][:, :, None]
    target = jnp.where(alive, places, places[:, :, :1]).reshape(-1)
    tile_rows, tile_cols = words * n_z, words * n_row_axis
    n_col, n_row = tile_cols // LANES, tile_rows // LANES
    order, spots, offsets = sort_slots(target, core, n_col)
    col_blocks = lax.all_gather(col_emb, ROW, axis=0)
    row_emb_late, col_blocks, order, spots, offsets = lax.optimization_barrier(
        (row_emb, col_blocks, order, spots, offsets)
    )
    row_blocks = lax.all_gather(row_emb_late, "col", axis=0)
    sub_rows, sub_cols = blocks.shape[5:]
    slots_each = blocks.shape[4]
    arrived = lax.all_to_all(
        blocks.reshape(-1, slots_each, sub_rows, sub_cols), ALL, split_axis=0, concat_axis=0, tiled=True
    ).reshape(-1, sub_rows, sub_cols)
    counts, part = place(
        pltpu.with_memory_space_constraint(target, pltpu.HBM), alive.astype(jnp.int32).reshape(-1), arrived, tile_rows // sub_rows, n_col
    )
    row_part = part[n_col:]
    row_part = swap_sum(row_part, "col", n_z, 1)
    row_part = swap_sum(row_part, "col", n_z, 2)
    row_part, col_blocks = lax.optimization_barrier((row_part, col_blocks))
    row_part = swap_sum(row_part, "col", n_z, 4)
    far_stack = stack_cols(core, col_blocks, padded, False)
    row_part, far_stack = lax.optimization_barrier((row_part, far_stack))
    col_part = jnp.concatenate([part[:n_col], row_part[n_row:]], axis=0)
    col_part = swap_sum(col_part, "core", CORES, 1)
    col_part, far_stack, col_blocks = lax.optimization_barrier((col_part, far_stack, col_blocks))
    col_part = swap_sum(col_part, "y", GRID_Y, 1)
    far_stack = stack_cols(core, col_blocks, padded, False, far_stack)
    col_part, far_stack, col_blocks = lax.optimization_barrier((col_part, far_stack, col_blocks))
    col_part = swap_sum(col_part, "y", GRID_Y, 2)
    near_stack = stack_cols(core, col_blocks, padded, True)
    col_part, near_stack, col_blocks = lax.optimization_barrier((col_part, near_stack, col_blocks))
    col_part = swap_sum(col_part, "x", GRID_X, 1)
    near_stack = stack_cols(core, col_blocks, padded, True, near_stack)
    col_part, near_stack = lax.optimization_barrier((col_part, near_stack))
    col_part, row_blocks = lax.optimization_barrier((col_part, row_blocks))
    row_stack, row_turned = turn(row_blocks, padded, deep)
    col_part = swap_sum(col_part, "x", GRID_X, 2)
    masses = jnp.concatenate([col_part[:n_col], row_part[:n_row], col_part[n_col:]], axis=0)
    scalars = (order, spots, offsets, core)
    chunks = n_col // CORES // BLOCKS
    early = chunks // 2
    inputs = (scalars, row_turned, row_stack)
    far_term, row_term = part_grads(*inputs, far_stack, counts, masses, None, 0, chunks)
    swapped = lax.ppermute(far_term, "core", [(0, 1), (1, 0)])
    piece, row_term = part_grads(*inputs, near_stack, counts, masses, row_term, 0, early)
    half, row_term = part_grads(
        *inputs, near_stack, counts, masses, row_term, early, chunks - early, (piece, swapped)
    )
    row_grad = lax.psum_scatter(row_term, "col", scatter_dimension=0, tiled=False)
    col_grad = jnp.sum(lax.all_to_all(half, ("x", "y"), split_axis=0, concat_axis=0, tiled=True), axis=0)
    loss_scale = 4.0 * float(words * n_z * n_row_axis) ** (-0.5)
    row_share = row_grad[:dim] * loss_scale
    col_share = col_grad[:dim] * loss_scale
    new_row_acc = row_acc + row_share * row_share
    new_col_acc = col_acc + col_share * col_share
    new_row_emb = row_emb - LEARNING_RATE * row_share / jnp.sqrt(new_row_acc)
    new_col_emb = col_emb - LEARNING_RATE * col_share / jnp.sqrt(new_col_acc)
    return (new_row_emb, new_col_emb, new_row_acc, new_col_acc)


def solution(mesh):
    n_z = mesh.devices.shape[1]
    inner = Mesh(mesh.devices.reshape(GRID_X, GRID_Y, CORES, n_z), ROW + ("col",))
    row_words = P(None, ROW + ("col",))
    col_words = P(None, ("col",) + ROW)
    return jax.shard_map(
        per_device,
        mesh=inner,
        in_specs=(P(ROW, "col"), P(ROW, "col"), P(ROW, "col"), row_words, col_words, row_words, col_words),
        out_specs=(row_words, col_words, row_words, col_words),
        check_vma=False,
    )
```

```python
import functools

import jax
import jax.numpy as jnp
from jax import lax
from jax.experimental import pallas as pl
from jax.experimental.pallas import tpu as pltpu
from jax.sharding import Mesh, PartitionSpec as P

LEARNING_RATE = 0.2
GRID_X, GRID_Y, CORES = 4, 4, 2
ROW = ("x", "y", "core")
ALL = ("col", "x", "y", "core")
LANES = 128
BLOCKS = 8
F32 = jnp.float32
BF16 = jnp.bfloat16


def split(value):
    high = value.astype(BF16)
    return high, (value - high.astype(F32)).astype(BF16)


def place_kernel(target, alive, arrived, counts_out, mass_out, dense, row_sums, col_sums):
    slots = arrived.shape[0]
    columns = col_sums.shape[0]
    shift = columns.bit_length() - 1
    row_words = row_sums.shape[0] // LANES * 8
    row_sums[...] = jnp.zeros(row_sums.shape, F32)
    col_sums[...] = jnp.zeros(col_sums.shape, F32)
    blank = jnp.zeros(arrived.shape[1:], F32)

    def clear(p, carry):
        dense[target[p]] = blank
        return carry

    lax.fori_loop(0, slots, clear, 0, unroll=8)

    def add(p, carry):
        place = target[p]
        value = jnp.where(alive[p] > 0, arrived[p], 0.0)
        row, column = lax.shift_right_logical(place, shift), place & (columns - 1)
        dense[place] = dense[place] + value
        row_sums[row] = row_sums[row] + value
        col_sums[column] = col_sums[column] + value
        return carry

    lax.fori_loop(0, slots, add, 0, unroll=8)

    def read(p, carry):
        counts_out[p] = dense[target[p]]
        return carry

    lax.fori_loop(0, slots, read, 0, unroll=8)
    col_part = jnp.sum(col_sums[...], axis=1)
    mass_out[0:columns, :] = col_part
    row_part = lax.dot_general(
        jnp.ones((8, LANES), F32),
        row_sums[...].reshape(-1, LANES),
        (((1,), (1,)), ((), ())),
        precision=lax.Precision.HIGHEST,
        preferred_element_type=F32,
    )
    for i in range(row_words):
        mass_out[columns + i : columns + i + 1, :] = row_part[0:1, i * LANES : (i + 1) * LANES]
    mass_out[columns + row_words :, :] = jnp.full((8, LANES), jnp.sum(col_part), F32)


def whole(count):
    return [pl.BlockSpec(memory_space=pltpu.VMEM)] * count


def place(target, alive, arrived, grid_rows, grid_columns):
    slots = arrived.shape[0]
    return pl.pallas_call(
        place_kernel,
        name="place_counts",
        grid_spec=pltpu.PrefetchScalarGridSpec(
            num_scalar_prefetch=2,
            grid=(1,),
            in_specs=whole(1),
            out_specs=whole(2),
            scratch_shapes=[
                pltpu.VMEM((grid_rows * grid_columns, 8, LANES), F32),
                pltpu.VMEM((grid_rows, 8, LANES), F32),
                pltpu.VMEM((grid_columns, 8, LANES), F32),
            ],
        ),
        out_shape=[
            jax.ShapeDtypeStruct((slots, 8, LANES), F32),
            jax.ShapeDtypeStruct((grid_columns + grid_rows * 8 // LANES + 8, LANES), F32),
        ],
        compiler_params=pltpu.CompilerParams(vmem_limit_bytes=22 << 20),
    )(target, alive, arrived)


def chunk_of(place, core, columns):
    column = place & (columns - 1)
    seat = lax.shift_right_logical(column, 1)
    far = (column & 1) ^ core
    chunk = (1 - far) * (columns // 2 // BLOCKS) + lax.shift_right_logical(seat, BLOCKS.bit_length() - 1)
    return chunk, seat & (BLOCKS - 1)


def sort_kernel(target, core, order, spots, offsets, cursor, *, columns):
    slots = target.shape[0]
    chunks = columns // BLOCKS
    for k in range(chunks + 1):
        cursor[k] = 0

    def count(p, carry):
        k = chunk_of(target[p], core[0], columns)[0]
        cursor[k] = cursor[k] + 1
        return carry

    lax.fori_loop(0, slots, count, 0, unroll=4)
    first = jnp.int32(0)
    for k in range(chunks):
        size = cursor[k]
        offsets[k] = first
        cursor[k] = first
        first = first + size
    offsets[chunks] = first

    def drop(p, carry):
        place = target[p]
        k, seat = chunk_of(place, core[0], columns)
        at = cursor[k]
        order[at] = p
        spots[at] = lax.shift_right_logical(place, columns.bit_length() - 1) * BLOCKS + seat
        cursor[k] = at + 1
        return carry

    lax.fori_loop(0, slots, drop, 0, unroll=4)


def sort_slots(target, core, columns):
    chunks = columns // BLOCKS
    smem = pl.BlockSpec(memory_space=pltpu.SMEM)
    return pl.pallas_call(
        functools.partial(sort_kernel, columns=columns),
        name="sort_slots",
        in_specs=[smem, smem],
        out_specs=[smem] * 3,
        out_shape=[
            jax.ShapeDtypeStruct(target.shape, jnp.int32),
            jax.ShapeDtypeStruct(target.shape, jnp.int32),
            jax.ShapeDtypeStruct((chunks + 1,), jnp.int32),
        ],
        scratch_shapes=[pltpu.SMEM((chunks + 1,), jnp.int32)],
    )(target, core)


def taller(value, padded):
    return jnp.concatenate([value, jnp.zeros((padded - value.shape[0], LANES), F32)], axis=0)


def turn_kernel(row_blocks, row_stack, row_turned):
    padded = row_stack.shape[0] // 2
    deep = row_turned.shape[1]
    for i in range(row_blocks.shape[0]):
        high, low = split(taller(row_blocks[i], padded))
        here = slice(i * LANES, (i + 1) * LANES)
        row_stack[0:padded, here] = high
        row_stack[padded:, here] = low
        high32, low32 = high.astype(F32), low.astype(F32)
        tall = jnp.concatenate(
            [high32, high32, low32, jnp.zeros((deep - 3 * padded, LANES), F32)], axis=0
        )
        row_turned[here, :] = (0.5 * tall.T).astype(BF16)


def turn(row_blocks, padded, deep):
    words = row_blocks.shape[0] * LANES
    return pl.pallas_call(
        turn_kernel,
        name="turn_rows",
        in_specs=whole(1),
        out_specs=whole(2),
        out_shape=[
            jax.ShapeDtypeStruct((2 * padded, words), BF16),
            jax.ShapeDtypeStruct((words, deep), BF16),
        ],
        compiler_params=pltpu.CompilerParams(vmem_limit_bytes=24 << 20),
    )(row_blocks)


def stack_kernel(core, col_blocks, *rest):
    out = rest[-1]
    dim = out.shape[0] // 2
    for i in range(col_blocks.shape[0]):
        high, low = split(taller(col_blocks[i, 0], dim))
        here = slice(i * LANES, (i + 1) * LANES)
        out[0:dim, here] = high
        out[dim:, here] = low


def stack_cols(core, col_blocks, padded, near, earlier=None):
    n_col, dim, _ = col_blocks.shape
    seats = n_col // CORES
    step = BLOCKS // 2
    first = 0 if earlier is None else seats // step // 2
    ready = [] if earlier is None else [earlier]
    col_blocks = pltpu.with_memory_space_constraint(col_blocks.reshape(seats, CORES, dim, LANES), pltpu.HBM)
    pick = lambda g, core: (first + g, core[0] if near else 1 - core[0], 0, 0)
    return pl.pallas_call(
        stack_kernel,
        name="stack_near" if near else "stack_far",
        grid_spec=pltpu.PrefetchScalarGridSpec(
            num_scalar_prefetch=1,
            grid=(seats // step // 2,),
            in_specs=[pl.BlockSpec((step, 1, dim, LANES), pick)]
            + [pl.BlockSpec(memory_space=pltpu.HBM)] * len(ready),
            out_specs=pl.BlockSpec((2 * padded, step * LANES), lambda g, *_: (0, first + g)),
        ),
        out_shape=pltpu.HBM((2 * padded, seats * LANES), BF16),
        input_output_aliases={2: 0} if ready else {},
        compiler_params=pltpu.CompilerParams(vmem_limit_bytes=14 << 20),
    )(core, col_blocks, *ready)


def part_kernel(
    order, spots, offsets, core, row_turned, row_stack, stack_far, counts_far, masses, *rest, near, first, merge
):
    merging = []
    if merge:
        *merging, rest = rest[1], rest[2], *rest[-2:], rest[:1] + rest[3:-2]
    col_term, row_term, scores, grads, row_bias, col_bias, counts, stacks = rest[-10:-2]
    arrival, stack_arrivals = rest[-2:]
    padded, n_row = row_term.shape[1], row_term.shape[0]
    n_col = col_bias.shape[0]
    step = pl.program_id(0)
    ct = step + first
    half_chunks = n_col // CORES // BLOCKS
    side = core[0] if near else 1 - core[0]

    width = BLOCKS * LANES
    fetch = pltpu.make_async_copy(counts_far, counts, arrival)

    def bring(chunk):
        cols = pl.ds(pl.multiple_of((first + chunk) * width, width), width)
        kept = stacks.at[chunk, pl.ds(0, 2 * padded), :]
        return pltpu.make_async_copy(stack_far.at[:, cols], kept, stack_arrivals.at[chunk])

    @pl.when(step == 0)
    def _():
        bring(0).start()
        fetch.start()
        for chunk in range(1, stacks.shape[0]):
            bring(chunk).start()
        log_total = jnp.log(masses[n_col + n_row : n_col + n_row + 1, :])
        col_bias[...] = 0.5 * (jnp.log(masses[0:n_col, :]) - log_total)
        row_logs = 0.5 * jnp.log(masses[n_col : n_col + n_row, :])
        for i in range(n_row):
            turned = jnp.broadcast_to(row_logs[i : i + 1, :], (LANES, LANES)).T
            row_bias[i * LANES // 8 : (i + 1) * LANES // 8] = turned.reshape(-1, 8, LANES)
        row_term[...] = rest[0][...] if near else jnp.zeros(row_term.shape, F32)

    bring(step).wait()
    stacks[step, 2 * padded : 3 * padded, :] = stacks[step, 0:padded, :]
    stacks[step, 3 * padded :, :] = jnp.zeros((stacks.shape[1] - 3 * padded, width), BF16)
    product = jnp.dot(row_turned[...], stacks[step], preferred_element_type=F32)
    for k in range(BLOCKS):
        bias = col_bias[pl.ds((ct * BLOCKS + k) * 2 + side, 1), :]
        value = product[:, k * LANES : (k + 1) * LANES].reshape(-1, 8, LANES) + row_bias[...] + bias
        scores[:, k] = value
        grads[:, k] = 0.5 * jnp.tanh(value) + 0.5
    here = ct + (half_chunks if near else 0)
    begin = offsets[here]
    end = offsets[here + 1]

    @pl.when(step == 0)
    def _():
        fetch.wait()

    def counted(group, carry):
        found = []
        for u in range(8):
            at = jnp.minimum(begin + group * 8 + u, end - 1)
            spot = spots[at]
            row, k = lax.shift_right_logical(spot, BLOCKS.bit_length() - 1), spot & (BLOCKS - 1)
            count = counts[order[at]]
            fresh = (0.1 + 0.25 * jnp.sqrt(count)) * (2.0 * scores[row, k] - jnp.log(count))
            found.append((row, k, fresh))
        for row, k, fresh in found:
            grads[row, k] = fresh
        return carry

    lax.fori_loop(0, lax.shift_right_logical(end - begin + 7, 3), counted, 0)
    if merge:
        piece, swapped, merged, leaves = merging
        merged[0 : first * BLOCKS] = swapped[0 : first * BLOCKS] + piece[...]
        parts = [pl.ds(0, first * BLOCKS), pl.ds(first * BLOCKS, BLOCKS)]
        leave = [
            pltpu.make_async_copy(merged.at[part], col_term.at[part], leaves.at[i])
            for i, part in enumerate(parts)
        ]
        leave[0].start()
    pieces = [split(grads[:, k].reshape(-1, LANES)) for k in range(BLOCKS)]
    high = jnp.concatenate([piece[0] for piece in pieces], axis=1)
    low = jnp.concatenate([piece[1] for piece in pieces], axis=1)
    both = jnp.dot(row_stack[...], high, preferred_element_type=F32)
    rest_ = jnp.dot(row_stack[0:padded, :], low, preferred_element_type=F32)
    total = both[0:padded] + both[padded:] + rest_
    for k in range(BLOCKS):
        block = total[:, k * LANES : (k + 1) * LANES]
        if merge:
            merged[first * BLOCKS + k] = swapped[first * BLOCKS + k] + block
        else:
            col_term[k] = block
    if merge:
        leave[1].start()
    turned = (((1,), (1,)), ((), ()))
    both = lax.dot_general(stacks[step, 0 : 2 * padded, :], high, turned, preferred_element_type=F32)
    rest_ = lax.dot_general(stacks[step, 0:padded, :], low, turned, preferred_element_type=F32)
    total = both[0:padded] + both[padded:] + rest_
    for i in range(n_row):
        row_term[i] = row_term[i] + total[:, i * LANES : (i + 1) * LANES]
    if merge:
        for copy in leave:
            copy.wait()


def part_grads(scalars, row_turned, row_stack, col_stack, counts, masses, earlier, first, count, extra=()):
    words, deep = row_turned.shape
    padded = row_stack.shape[0] // 2
    blocks = col_stack.shape[1] // LANES
    near = earlier is not None
    merge = bool(extra)
    ready = [earlier] if near else []
    out_blocks = blocks if merge else count * BLOCKS
    scratch = [
        pltpu.VMEM((blocks, padded, LANES), F32),
        pltpu.SemaphoreType.DMA((2,)),
    ]
    return pl.pallas_call(
        functools.partial(part_kernel, near=near, first=first, merge=merge),
        name="merge_grads" if merge else "near_grads" if near else "far_grads",
        grid_spec=pltpu.PrefetchScalarGridSpec(
            num_scalar_prefetch=4,
            grid=(count,),
            in_specs=whole(2)
            + [pl.BlockSpec(memory_space=pltpu.HBM)] * 2
            + whole(1 + len(ready) + len(extra)),
            out_specs=[
                pl.BlockSpec(memory_space=pltpu.HBM)
                if merge
                else pl.BlockSpec((BLOCKS, padded, LANES), lambda g, *_: (g, 0, 0)),
                pl.BlockSpec((words // LANES, padded, LANES), lambda g, *_: (0, 0, 0)),
            ],
            scratch_shapes=[
                pltpu.VMEM((words // 8, BLOCKS, 8, LANES), F32),
                pltpu.VMEM((words // 8, BLOCKS, 8, LANES), F32),
                pltpu.VMEM((words // 8, 8, LANES), F32),
                pltpu.VMEM((blocks * CORES, LANES), F32),
                pltpu.VMEM(counts.shape, F32),
                pltpu.VMEM((count, deep, BLOCKS * LANES), BF16),
                pltpu.SemaphoreType.DMA(()),
                pltpu.SemaphoreType.DMA((count,)),
            ]
            + (scratch if merge else []),
        ),
        out_shape=[
            (pltpu.HBM if merge else jax.ShapeDtypeStruct)((out_blocks, padded, LANES), F32),
            (pltpu.HBM if merge else jax.ShapeDtypeStruct)((words // LANES, padded, LANES), F32),
        ],
        compiler_params=pltpu.CompilerParams(vmem_limit_bytes=40 << 20),
    )(*scalars, row_turned, row_stack, pltpu.with_memory_space_constraint(col_stack, pltpu.HBM), pltpu.with_memory_space_constraint(counts, pltpu.HBM), masses, *ready, *extra)


def swap_sum(value, axis, size, bit):
    return value + lax.ppermute(value, axis, [(i, i ^ bit) for i in range(size)])


def per_device(blocks, plan, live, row_emb, col_emb, row_acc, col_acc):
    n_z = lax.axis_size("col")
    n_row_axis = GRID_X * GRID_Y * CORES
    dim, words = row_emb.shape
    padded = -(-dim // 16) * 16
    deep = -(-3 * padded // 256) * 256
    core = lax.axis_index("core").astype(jnp.int32).reshape(1)
    places = plan[0, 0]
    alive = lax.broadcasted_iota(jnp.int32, places.shape, 2) < live[0, 0][:, :, None]
    target = jnp.where(alive, places, places[:, :, :1]).reshape(-1)
    tile_rows, tile_cols = words * n_z, words * n_row_axis
    n_col, n_row = tile_cols // LANES, tile_rows // LANES
    order, spots, offsets = sort_slots(target, core, n_col)
    col_blocks = lax.all_gather(col_emb, ROW, axis=0)
    row_emb_late, col_blocks, order, spots, offsets = lax.optimization_barrier(
        (row_emb, col_blocks, order, spots, offsets)
    )
    row_blocks = lax.all_gather(row_emb_late, "col", axis=0)
    sub_rows, sub_cols = blocks.shape[5:]
    slots_each = blocks.shape[4]
    arrived = lax.all_to_all(
        blocks.reshape(-1, slots_each, sub_rows, sub_cols), ALL, split_axis=0, concat_axis=0, tiled=True
    ).reshape(-1, sub_rows, sub_cols)
    counts, part = place(
        pltpu.with_memory_space_constraint(target, pltpu.HBM), alive.astype(jnp.int32).reshape(-1), arrived, tile_rows // sub_rows, n_col
    )
    row_part = part[n_col:]
    row_part = swap_sum(row_part, "col", n_z, 1)
    row_part = swap_sum(row_part, "col", n_z, 2)
    row_part, col_blocks = lax.optimization_barrier((row_part, col_blocks))
    row_part = swap_sum(row_part, "col", n_z, 4)
    far_stack = stack_cols(core, col_blocks, padded, False)
    row_part, far_stack = lax.optimization_barrier((row_part, far_stack))
    col_part = jnp.concatenate([part[:n_col], row_part[n_row:]], axis=0)
    col_part = swap_sum(col_part, "core", CORES, 1)
    col_part, far_stack, col_blocks = lax.optimization_barrier((col_part, far_stack, col_blocks))
    col_part = swap_sum(col_part, "y", GRID_Y, 1)
    far_stack = stack_cols(core, col_blocks, padded, False, far_stack)
    col_part, far_stack, col_blocks = lax.optimization_barrier((col_part, far_stack, col_blocks))
    col_part = swap_sum(col_part, "y", GRID_Y, 2)
    near_stack = stack_cols(core, col_blocks, padded, True)
    col_part, near_stack, col_blocks = lax.optimization_barrier((col_part, near_stack, col_blocks))
    col_part = swap_sum(col_part, "x", GRID_X, 1)
    near_stack = stack_cols(core, col_blocks, padded, True, near_stack)
    col_part, near_stack = lax.optimization_barrier((col_part, near_stack))
    col_part, row_blocks = lax.optimization_barrier((col_part, row_blocks))
    row_stack, row_turned = turn(row_blocks, padded, deep)
    col_part = swap_sum(col_part, "x", GRID_X, 2)
    masses = jnp.concatenate([col_part[:n_col], row_part[:n_row], col_part[n_col:]], axis=0)
    scalars = (order, spots, offsets, core)
    chunks = n_col // CORES // BLOCKS
    early = chunks // 2
    inputs = (scalars, row_turned, row_stack)
    far_term, row_term = part_grads(*inputs, far_stack, counts, masses, None, 0, chunks)
    swapped = lax.ppermute(far_term, "core", [(0, 1), (1, 0)])
    piece, row_term = part_grads(*inputs, near_stack, counts, masses, row_term, 0, early)
    half, row_term = part_grads(
        *inputs, near_stack, counts, masses, row_term, early, chunks - early, (piece, swapped)
    )
    loss_scale = 4.0 * float(words * n_z * n_row_axis) ** (-0.5)
    row_grad = lax.psum_scatter(row_term, "col", scatter_dimension=0, tiled=False)
    arrived_cols = lax.all_to_all(half, ("x", "y"), split_axis=0, concat_axis=0, tiled=True)
    row_share = row_grad[:dim] * loss_scale
    new_row_acc = row_acc + row_share * row_share
    new_row_emb = row_emb - LEARNING_RATE * row_share / jnp.sqrt(new_row_acc)
    arrived_cols, new_row_acc, new_row_emb = lax.optimization_barrier((arrived_cols, new_row_acc, new_row_emb))
    col_share = jnp.sum(arrived_cols, axis=0)[:dim] * loss_scale
    new_col_acc = col_acc + col_share * col_share
    new_col_emb = col_emb - LEARNING_RATE * col_share / jnp.sqrt(new_col_acc)
    return (new_row_emb, new_col_emb, new_row_acc, new_col_acc)

def solution(mesh):
    n_z = mesh.devices.shape[1]
    inner = Mesh(mesh.devices.reshape(GRID_X, GRID_Y, CORES, n_z), ROW + ("col",))
    row_words = P(None, ROW + ("col",))
    col_words = P(None, ("col",) + ROW)
    return jax.shard_map(
        per_device,
        mesh=inner,
        in_specs=(P(ROW, "col"), P(ROW, "col"), P(ROW, "col"), row_words, col_words, row_words, col_words),
        out_specs=(row_words, col_words, row_words, col_words),
        check_vma=False,
    )
```

```python
import functools

import jax
import jax.numpy as jnp
from jax import lax
from jax.experimental import pallas as pl
from jax.experimental.pallas import tpu as pltpu
from jax.sharding import Mesh, PartitionSpec as P

LEARNING_RATE = 0.2
GRID_X, GRID_Y, CORES = 4, 4, 2
ROW = ("x", "y", "core")
ALL = ("col", "x", "y", "core")
LANES = 128
BLOCKS = 8
F32 = jnp.float32
BF16 = jnp.bfloat16


def split(value):
    high = value.astype(BF16)
    return high, (value - high.astype(F32)).astype(BF16)


def place_kernel(target, alive, arrived, counts_out, mass_out, dense, row_sums, col_sums):
    slots = arrived.shape[0]
    columns = col_sums.shape[0]
    shift = columns.bit_length() - 1
    row_words = row_sums.shape[0] // LANES * 8
    row_sums[...] = jnp.zeros(row_sums.shape, F32)
    col_sums[...] = jnp.zeros(col_sums.shape, F32)
    blank = jnp.zeros(arrived.shape[1:], F32)

    def clear(p, carry):
        dense[target[p]] = blank
        return carry

    lax.fori_loop(0, slots, clear, 0, unroll=8)

    def add(p, carry):
        place = target[p]
        value = jnp.where(alive[p] > 0, arrived[p], 0.0)
        row, column = lax.shift_right_logical(place, shift), place & (columns - 1)
        dense[place] = dense[place] + value
        row_sums[row] = row_sums[row] + value
        col_sums[column] = col_sums[column] + value
        return carry

    lax.fori_loop(0, slots, add, 0, unroll=8)

    def read(p, carry):
        counts_out[p] = dense[target[p]]
        return carry

    lax.fori_loop(0, slots, read, 0, unroll=8)
    col_part = jnp.sum(col_sums[...], axis=1)
    mass_out[0:columns, :] = col_part
    row_part = lax.dot_general(
        jnp.ones((8, LANES), F32),
        row_sums[...].reshape(-1, LANES),
        (((1,), (1,)), ((), ())),
        precision=lax.Precision.HIGHEST,
        preferred_element_type=F32,
    )
    for i in range(row_words):
        mass_out[columns + i : columns + i + 1, :] = row_part[0:1, i * LANES : (i + 1) * LANES]
    mass_out[columns + row_words :, :] = jnp.full((8, LANES), jnp.sum(col_part), F32)


def whole(count):
    return [pl.BlockSpec(memory_space=pltpu.VMEM)] * count


def place(target, alive, arrived, grid_rows, grid_columns):
    slots = arrived.shape[0]
    return pl.pallas_call(
        place_kernel,
        name="place_counts",
        grid_spec=pltpu.PrefetchScalarGridSpec(
            num_scalar_prefetch=2,
            grid=(1,),
            in_specs=whole(1),
            out_specs=whole(2),
            scratch_shapes=[
                pltpu.VMEM((grid_rows * grid_columns, 8, LANES), F32),
                pltpu.VMEM((grid_rows, 8, LANES), F32),
                pltpu.VMEM((grid_columns, 8, LANES), F32),
            ],
        ),
        out_shape=[
            jax.ShapeDtypeStruct((slots, 8, LANES), F32),
            jax.ShapeDtypeStruct((grid_columns + grid_rows * 8 // LANES + 8, LANES), F32),
        ],
        compiler_params=pltpu.CompilerParams(vmem_limit_bytes=22 << 20),
    )(target, alive, arrived)


def chunk_of(place, core, columns):
    column = place & (columns - 1)
    seat = lax.shift_right_logical(column, 1)
    far = (column & 1) ^ core
    chunk = (1 - far) * (columns // 2 // BLOCKS) + lax.shift_right_logical(seat, BLOCKS.bit_length() - 1)
    return chunk, seat & (BLOCKS - 1)


def sort_kernel(target, core, order, spots, offsets, cursor, *, columns):
    slots = target.shape[0]
    chunks = columns // BLOCKS
    for k in range(chunks + 1):
        cursor[k] = 0

    def count(p, carry):
        k = chunk_of(target[p], core[0], columns)[0]
        cursor[k] = cursor[k] + 1
        return carry

    lax.fori_loop(0, slots, count, 0, unroll=4)
    first = jnp.int32(0)
    for k in range(chunks):
        size = cursor[k]
        offsets[k] = first
        cursor[k] = first
        first = first + size
    offsets[chunks] = first

    def drop(p, carry):
        place = target[p]
        k, seat = chunk_of(place, core[0], columns)
        at = cursor[k]
        order[at] = p
        spots[at] = lax.shift_right_logical(place, columns.bit_length() - 1) * BLOCKS + seat
        cursor[k] = at + 1
        return carry

    lax.fori_loop(0, slots, drop, 0, unroll=4)


def sort_slots(target, core, columns):
    chunks = columns // BLOCKS
    smem = pl.BlockSpec(memory_space=pltpu.SMEM)
    return pl.pallas_call(
        functools.partial(sort_kernel, columns=columns),
        name="sort_slots",
        in_specs=[smem, smem],
        out_specs=[smem] * 3,
        out_shape=[
            jax.ShapeDtypeStruct(target.shape, jnp.int32),
            jax.ShapeDtypeStruct(target.shape, jnp.int32),
            jax.ShapeDtypeStruct((chunks + 1,), jnp.int32),
        ],
        scratch_shapes=[pltpu.SMEM((chunks + 1,), jnp.int32)],
    )(target, core)


def taller(value, padded):
    return jnp.concatenate([value, jnp.zeros((padded - value.shape[0], LANES), F32)], axis=0)


def turn_kernel(row_blocks, row_stack, row_turned):
    padded = row_stack.shape[0] // 2
    deep = row_turned.shape[1]
    for i in range(row_blocks.shape[0]):
        high, low = split(taller(row_blocks[i], padded))
        here = slice(i * LANES, (i + 1) * LANES)
        row_stack[0:padded, here] = high
        row_stack[padded:, here] = low
        high32, low32 = high.astype(F32), low.astype(F32)
        tall = jnp.concatenate(
            [high32, high32, low32, jnp.zeros((deep - 3 * padded, LANES), F32)], axis=0
        )
        row_turned[here, :] = (0.5 * tall.T).astype(BF16)


def turn(row_blocks, padded, deep):
    words = row_blocks.shape[0] * LANES
    return pl.pallas_call(
        turn_kernel,
        name="turn_rows",
        in_specs=whole(1),
        out_specs=whole(2),
        out_shape=[
            jax.ShapeDtypeStruct((2 * padded, words), BF16),
            jax.ShapeDtypeStruct((words, deep), BF16),
        ],
        compiler_params=pltpu.CompilerParams(vmem_limit_bytes=24 << 20),
    )(row_blocks)


def stack_kernel(core, col_blocks, *rest):
    out = rest[-1]
    dim = out.shape[0] // 2
    for i in range(col_blocks.shape[0]):
        high, low = split(taller(col_blocks[i, 0], dim))
        here = slice(i * LANES, (i + 1) * LANES)
        out[0:dim, here] = high
        out[dim:, here] = low


def stack_cols(core, col_blocks, padded, near, earlier=None):
    n_col, dim, _ = col_blocks.shape
    seats = n_col // CORES
    step = BLOCKS // 2
    first = 0 if earlier is None else seats // step // 2
    ready = [] if earlier is None else [earlier]
    col_blocks = pltpu.with_memory_space_constraint(col_blocks.reshape(seats, CORES, dim, LANES), pltpu.HBM)
    pick = lambda g, core: (first + g, core[0] if near else 1 - core[0], 0, 0)
    return pl.pallas_call(
        stack_kernel,
        name="stack_near" if near else "stack_far",
        grid_spec=pltpu.PrefetchScalarGridSpec(
            num_scalar_prefetch=1,
            grid=(seats // step // 2,),
            in_specs=[pl.BlockSpec((step, 1, dim, LANES), pick)]
            + [pl.BlockSpec(memory_space=pltpu.HBM)] * len(ready),
            out_specs=pl.BlockSpec((2 * padded, step * LANES), lambda g, *_: (0, first + g)),
        ),
        out_shape=pltpu.HBM((2 * padded, seats * LANES), BF16),
        input_output_aliases={2: 0} if ready else {},
        compiler_params=pltpu.CompilerParams(vmem_limit_bytes=14 << 20),
    )(core, col_blocks, *ready)


def part_kernel(
    order, spots, offsets, core, row_turned, row_stack, stack_far, counts_far, masses, *rest, near, first, merge
):
    merging = []
    if merge:
        *merging, rest = rest[1], rest[2], *rest[-2:], rest[:1] + rest[3:-2]
    col_term, row_term, scores, grads, row_bias, col_bias, counts, stacks = rest[-10:-2]
    arrival, stack_arrivals = rest[-2:]
    padded, n_row = row_term.shape[1], row_term.shape[0]
    n_col = col_bias.shape[0]
    step = pl.program_id(0)
    ct = step + first
    half_chunks = n_col // CORES // BLOCKS
    side = core[0] if near else 1 - core[0]

    width = BLOCKS * LANES
    fetch = pltpu.make_async_copy(counts_far, counts, arrival)

    def bring(chunk):
        cols = pl.ds(pl.multiple_of((first + chunk) * width, width), width)
        kept = stacks.at[chunk, pl.ds(0, 2 * padded), :]
        return pltpu.make_async_copy(stack_far.at[:, cols], kept, stack_arrivals.at[chunk])

    @pl.when(step == 0)
    def _():
        if not near:
            bring(0).start()
            fetch.start()
            for chunk in range(1, stacks.shape[0]):
                bring(chunk).start()
        log_total = jnp.log(masses[n_col + n_row : n_col + n_row + 1, :])
        col_bias[...] = 0.5 * (jnp.log(masses[0:n_col, :]) - log_total)
        row_logs = 0.5 * jnp.log(masses[n_col : n_col + n_row, :])
        for i in range(n_row):
            turned = jnp.broadcast_to(row_logs[i : i + 1, :], (LANES, LANES)).T
            row_bias[i * LANES // 8 : (i + 1) * LANES // 8] = turned.reshape(-1, 8, LANES)
        row_term[...] = rest[0][...] if near else jnp.zeros(row_term.shape, F32)

    if near:
        stacks[step, 0 : 2 * padded, :] = stack_far[:, first * width : (first + 1) * width]
    else:
        bring(step).wait()
    stacks[step, 2 * padded : 3 * padded, :] = stacks[step, 0:padded, :]
    stacks[step, 3 * padded :, :] = jnp.zeros((stacks.shape[1] - 3 * padded, width), BF16)
    product = jnp.dot(row_turned[...], stacks[step], preferred_element_type=F32)
    for k in range(BLOCKS):
        bias = col_bias[pl.ds((ct * BLOCKS + k) * 2 + side, 1), :]
        value = product[:, k * LANES : (k + 1) * LANES].reshape(-1, 8, LANES) + row_bias[...] + bias
        scores[:, k] = value
        grads[:, k] = 0.5 * jnp.tanh(value) + 0.5
    here = ct + (half_chunks if near else 0)
    begin = offsets[here]
    end = offsets[here + 1]

    if not near:

        @pl.when(step == 0)
        def _():
            fetch.wait()

    def counted(group, carry):
        found = []
        for u in range(8):
            at = jnp.minimum(begin + group * 8 + u, end - 1)
            spot = spots[at]
            row, k = lax.shift_right_logical(spot, BLOCKS.bit_length() - 1), spot & (BLOCKS - 1)
            count = (counts_far if near else counts)[order[at]]
            fresh = (0.1 + 0.25 * jnp.sqrt(count)) * (2.0 * scores[row, k] - jnp.log(count))
            found.append((row, k, fresh))
        for row, k, fresh in found:
            grads[row, k] = fresh
        return carry

    lax.fori_loop(0, lax.shift_right_logical(end - begin + 7, 3), counted, 0)
    if merge:
        piece, swapped, merged, leaves = merging
        merged[0 : first * BLOCKS] = swapped[0 : first * BLOCKS] + piece[...]
        parts = [pl.ds(0, first * BLOCKS), pl.ds(first * BLOCKS, BLOCKS)]
        leave = [
            pltpu.make_async_copy(merged.at[part], col_term.at[part], leaves.at[i])
            for i, part in enumerate(parts)
        ]
        leave[0].start()
    pieces = [split(grads[:, k].reshape(-1, LANES)) for k in range(BLOCKS)]
    high = jnp.concatenate([piece[0] for piece in pieces], axis=1)
    low = jnp.concatenate([piece[1] for piece in pieces], axis=1)
    both = jnp.dot(row_stack[...], high, preferred_element_type=F32)
    rest_ = jnp.dot(row_stack[0:padded, :], low, preferred_element_type=F32)
    total = both[0:padded] + both[padded:] + rest_
    for k in range(BLOCKS):
        block = total[:, k * LANES : (k + 1) * LANES]
        if merge:
            merged[first * BLOCKS + k] = swapped[first * BLOCKS + k] + block
        else:
            col_term[k] = block
    if merge:
        leave[1].start()
    turned = (((1,), (1,)), ((), ()))
    both = lax.dot_general(stacks[step, 0 : 2 * padded, :], high, turned, preferred_element_type=F32)
    rest_ = lax.dot_general(stacks[step, 0:padded, :], low, turned, preferred_element_type=F32)
    total = both[0:padded] + both[padded:] + rest_
    for i in range(n_row):
        row_term[i] = row_term[i] + total[:, i * LANES : (i + 1) * LANES]
    if merge:
        for copy in leave:
            copy.wait()


def part_grads(scalars, row_turned, row_stack, col_stack, counts, masses, earlier, first, count, extra=()):
    words, deep = row_turned.shape
    padded = row_stack.shape[0] // 2
    blocks = col_stack.shape[1] // LANES
    near = earlier is not None
    merge = bool(extra)
    ready = [earlier] if near else []
    placed = (col_stack, counts) if near else [pltpu.with_memory_space_constraint(value, pltpu.HBM) for value in (col_stack, counts)]
    out_blocks = blocks if merge else count * BLOCKS
    scratch = [
        pltpu.VMEM((blocks, padded, LANES), F32),
        pltpu.SemaphoreType.DMA((2,)),
    ]
    return pl.pallas_call(
        functools.partial(part_kernel, near=near, first=first, merge=merge),
        name="merge_grads" if merge else "near_grads" if near else "far_grads",
        grid_spec=pltpu.PrefetchScalarGridSpec(
            num_scalar_prefetch=4,
            grid=(count,),
            in_specs=whole(2)
            + [pl.BlockSpec(memory_space=pltpu.VMEM if near else pltpu.HBM)] * 2
            + whole(1 + len(ready) + len(extra)),
            out_specs=[
                pl.BlockSpec(memory_space=pltpu.HBM)
                if merge
                else pl.BlockSpec((BLOCKS, padded, LANES), lambda g, *_: (g, 0, 0)),
                pl.BlockSpec((words // LANES, padded, LANES), lambda g, *_: (0, 0, 0)),
            ],
            scratch_shapes=[
                pltpu.VMEM((words // 8, BLOCKS, 8, LANES), F32),
                pltpu.VMEM((words // 8, BLOCKS, 8, LANES), F32),
                pltpu.VMEM((words // 8, 8, LANES), F32),
                pltpu.VMEM((blocks * CORES, LANES), F32),
                pltpu.VMEM((8, 8, LANES) if near else counts.shape, F32),
                pltpu.VMEM((count, deep, BLOCKS * LANES), BF16),
                pltpu.SemaphoreType.DMA(()),
                pltpu.SemaphoreType.DMA((count,)),
            ]
            + (scratch if merge else []),
        ),
        out_shape=[
            (pltpu.HBM if merge else jax.ShapeDtypeStruct)((out_blocks, padded, LANES), F32),
            (pltpu.HBM if merge else jax.ShapeDtypeStruct)((words // LANES, padded, LANES), F32),
        ],
        compiler_params=pltpu.CompilerParams(vmem_limit_bytes=36 << 20),
    )(*scalars, row_turned, row_stack, *placed, masses, *ready, *extra)


def swap_sum(value, axis, size, bit):
    return value + lax.ppermute(value, axis, [(i, i ^ bit) for i in range(size)])


def per_device(blocks, plan, live, row_emb, col_emb, row_acc, col_acc):
    n_z = lax.axis_size("col")
    n_row_axis = GRID_X * GRID_Y * CORES
    dim, words = row_emb.shape
    padded = -(-dim // 16) * 16
    deep = -(-3 * padded // 256) * 256
    core = lax.axis_index("core").astype(jnp.int32).reshape(1)
    places = plan[0, 0]
    alive = lax.broadcasted_iota(jnp.int32, places.shape, 2) < live[0, 0][:, :, None]
    target = jnp.where(alive, places, places[:, :, :1]).reshape(-1)
    tile_rows, tile_cols = words * n_z, words * n_row_axis
    n_col, n_row = tile_cols // LANES, tile_rows // LANES
    order, spots, offsets = sort_slots(target, core, n_col)
    col_blocks = lax.all_gather(col_emb, ROW, axis=0)
    row_emb_late, col_blocks, order, spots, offsets = lax.optimization_barrier(
        (row_emb, col_blocks, order, spots, offsets)
    )
    row_blocks = lax.all_gather(row_emb_late, "col", axis=0)
    sub_rows, sub_cols = blocks.shape[5:]
    slots_each = blocks.shape[4]
    arrived = lax.all_to_all(
        blocks.reshape(-1, slots_each, sub_rows, sub_cols), ALL, split_axis=0, concat_axis=0, tiled=True
    ).reshape(-1, sub_rows, sub_cols)
    counts, part = place(
        pltpu.with_memory_space_constraint(target, pltpu.HBM), alive.astype(jnp.int32).reshape(-1), arrived, tile_rows // sub_rows, n_col
    )
    row_part = part[n_col:]
    row_part = swap_sum(row_part, "col", n_z, 1)
    row_part = swap_sum(row_part, "col", n_z, 2)
    row_part, col_blocks = lax.optimization_barrier((row_part, col_blocks))
    row_part = swap_sum(row_part, "col", n_z, 4)
    far_stack = stack_cols(core, col_blocks, padded, False)
    row_part, far_stack = lax.optimization_barrier((row_part, far_stack))
    col_part = jnp.concatenate([part[:n_col], row_part[n_row:]], axis=0)
    col_part = swap_sum(col_part, "core", CORES, 1)
    col_part, far_stack, col_blocks = lax.optimization_barrier((col_part, far_stack, col_blocks))
    col_part = swap_sum(col_part, "y", GRID_Y, 1)
    far_stack = stack_cols(core, col_blocks, padded, False, far_stack)
    col_part, far_stack, col_blocks = lax.optimization_barrier((col_part, far_stack, col_blocks))
    col_part = swap_sum(col_part, "y", GRID_Y, 2)
    near_stack = stack_cols(core, col_blocks, padded, True)
    col_part, near_stack, col_blocks = lax.optimization_barrier((col_part, near_stack, col_blocks))
    col_part = swap_sum(col_part, "x", GRID_X, 1)
    near_stack = stack_cols(core, col_blocks, padded, True, near_stack)
    col_part, near_stack = lax.optimization_barrier((col_part, near_stack))
    col_part, row_blocks = lax.optimization_barrier((col_part, row_blocks))
    row_stack, row_turned = turn(row_blocks, padded, deep)
    col_part = swap_sum(col_part, "x", GRID_X, 2)
    masses = jnp.concatenate([col_part[:n_col], row_part[:n_row], col_part[n_col:]], axis=0)
    scalars = (order, spots, offsets, core)
    chunks = n_col // CORES // BLOCKS
    early = chunks // 2
    inputs = (scalars, row_turned, row_stack)
    far_term, row_term = part_grads(*inputs, far_stack, counts, masses, None, 0, chunks)
    swapped = lax.ppermute(far_term, "core", [(0, 1), (1, 0)])
    piece, row_term = part_grads(*inputs, near_stack, counts, masses, row_term, 0, early)
    half, row_term = part_grads(
        *inputs, near_stack, counts, masses, row_term, early, chunks - early, (piece, swapped)
    )
    loss_scale = 4.0 * float(words * n_z * n_row_axis) ** (-0.5)
    row_grad = lax.psum_scatter(row_term, "col", scatter_dimension=0, tiled=False)
    arrived_cols = lax.all_to_all(half, ("x", "y"), split_axis=0, concat_axis=0, tiled=True)
    row_share = row_grad[:dim] * loss_scale
    new_row_acc = row_acc + row_share * row_share
    new_row_emb = row_emb - LEARNING_RATE * row_share / jnp.sqrt(new_row_acc)
    arrived_cols, new_row_acc, new_row_emb = lax.optimization_barrier((arrived_cols, new_row_acc, new_row_emb))
    col_share = jnp.sum(arrived_cols, axis=0)[:dim] * loss_scale
    new_col_acc = col_acc + col_share * col_share
    new_col_emb = col_emb - LEARNING_RATE * col_share / jnp.sqrt(new_col_acc)
    return (new_row_emb, new_col_emb, new_row_acc, new_col_acc)

def solution(mesh):
    n_z = mesh.devices.shape[1]
    inner = Mesh(mesh.devices.reshape(GRID_X, GRID_Y, CORES, n_z), ROW + ("col",))
    row_words = P(None, ROW + ("col",))
    col_words = P(None, ("col",) + ROW)
    return jax.shard_map(
        per_device,
        mesh=inner,
        in_specs=(P(ROW, "col"), P(ROW, "col"), P(ROW, "col"), row_words, col_words, row_words, col_words),
        out_specs=(row_words, col_words, row_words, col_words),
        check_vma=False,
    )
```

```python
import functools

import jax
import jax.numpy as jnp
from jax import lax
from jax.experimental import pallas as pl
from jax.experimental.pallas import tpu as pltpu
from jax.sharding import Mesh, PartitionSpec as P

LEARNING_RATE = 0.2
GRID_X, GRID_Y, CORES = 4, 4, 2
ROW = ("x", "y", "core")
ALL = ("col", "x", "y", "core")
LANES = 128
BLOCKS = 8
F32 = jnp.float32
BF16 = jnp.bfloat16


def split(value):
    high = value.astype(BF16)
    return high, (value - high.astype(F32)).astype(BF16)


def place_kernel(target, alive, arrived, counts_out, mass_out, dense, row_sums, col_sums):
    slots = arrived.shape[0]
    columns = col_sums.shape[0]
    shift = columns.bit_length() - 1
    row_words = row_sums.shape[0] // LANES * 8
    row_sums[...] = jnp.zeros(row_sums.shape, F32)
    col_sums[...] = jnp.zeros(col_sums.shape, F32)
    blank = jnp.zeros(arrived.shape[1:], F32)

    def clear(p, carry):
        dense[target[p]] = blank
        return carry

    lax.fori_loop(0, slots, clear, 0, unroll=8)

    def add(p, carry):
        place = target[p]
        value = jnp.where(alive[p] > 0, arrived[p], 0.0)
        row, column = lax.shift_right_logical(place, shift), place & (columns - 1)
        dense[place] = dense[place] + value
        row_sums[row] = row_sums[row] + value
        col_sums[column] = col_sums[column] + value
        return carry

    lax.fori_loop(0, slots, add, 0, unroll=8)

    def read(p, carry):
        counts_out[p] = dense[target[p]]
        return carry

    lax.fori_loop(0, slots, read, 0, unroll=8)
    col_part = jnp.sum(col_sums[...], axis=1)
    mass_out[0:columns, :] = col_part
    row_part = lax.dot_general(
        jnp.ones((8, LANES), F32),
        row_sums[...].reshape(-1, LANES),
        (((1,), (1,)), ((), ())),
        precision=lax.Precision.HIGHEST,
        preferred_element_type=F32,
    )
    for i in range(row_words):
        mass_out[columns + i : columns + i + 1, :] = row_part[0:1, i * LANES : (i + 1) * LANES]
    mass_out[columns + row_words :, :] = jnp.full((8, LANES), jnp.sum(col_part), F32)


def whole(count):
    return [pl.BlockSpec(memory_space=pltpu.VMEM)] * count


def place(target, alive, arrived, grid_rows, grid_columns):
    slots = arrived.shape[0]
    return pl.pallas_call(
        place_kernel,
        name="place_counts",
        grid_spec=pltpu.PrefetchScalarGridSpec(
            num_scalar_prefetch=2,
            grid=(1,),
            in_specs=whole(1),
            out_specs=whole(2),
            scratch_shapes=[
                pltpu.VMEM((grid_rows * grid_columns, 8, LANES), F32),
                pltpu.VMEM((grid_rows, 8, LANES), F32),
                pltpu.VMEM((grid_columns, 8, LANES), F32),
            ],
        ),
        out_shape=[
            jax.ShapeDtypeStruct((slots, 8, LANES), F32),
            jax.ShapeDtypeStruct((grid_columns + grid_rows * 8 // LANES + 8, LANES), F32),
        ],
        compiler_params=pltpu.CompilerParams(vmem_limit_bytes=22 << 20),
    )(target, alive, arrived)


def chunk_of(place, core, columns):
    column = place & (columns - 1)
    seat = lax.shift_right_logical(column, 1)
    far = (column & 1) ^ core
    chunk = (1 - far) * (columns // 2 // BLOCKS) + lax.shift_right_logical(seat, BLOCKS.bit_length() - 1)
    return chunk, seat & (BLOCKS - 1)


def sort_kernel(target, core, order, spots, offsets, cursor, *, columns):
    slots = target.shape[0]
    chunks = columns // BLOCKS
    for k in range(chunks + 1):
        cursor[k] = 0

    def count(p, carry):
        k = chunk_of(target[p], core[0], columns)[0]
        cursor[k] = cursor[k] + 1
        return carry

    lax.fori_loop(0, slots, count, 0, unroll=4)
    first = jnp.int32(0)
    for k in range(chunks):
        size = cursor[k]
        offsets[k] = first
        cursor[k] = first
        first = first + size
    offsets[chunks] = first

    def drop(p, carry):
        place = target[p]
        k, seat = chunk_of(place, core[0], columns)
        at = cursor[k]
        order[at] = p
        spots[at] = lax.shift_right_logical(place, columns.bit_length() - 1) * BLOCKS + seat
        cursor[k] = at + 1
        return carry

    lax.fori_loop(0, slots, drop, 0, unroll=4)


def sort_slots(target, core, columns):
    chunks = columns // BLOCKS
    smem = pl.BlockSpec(memory_space=pltpu.SMEM)
    return pl.pallas_call(
        functools.partial(sort_kernel, columns=columns),
        name="sort_slots",
        in_specs=[smem, smem],
        out_specs=[smem] * 3,
        out_shape=[
            jax.ShapeDtypeStruct(target.shape, jnp.int32),
            jax.ShapeDtypeStruct(target.shape, jnp.int32),
            jax.ShapeDtypeStruct((chunks + 1,), jnp.int32),
        ],
        scratch_shapes=[pltpu.SMEM((chunks + 1,), jnp.int32)],
    )(target, core)


def taller(value, padded):
    return jnp.concatenate([value, jnp.zeros((padded - value.shape[0], LANES), F32)], axis=0)


def turn_kernel(row_blocks, row_stack, row_turned):
    padded = row_stack.shape[0] // 2
    deep = row_turned.shape[1]
    for i in range(row_blocks.shape[0]):
        high, low = split(taller(row_blocks[i], padded))
        here = slice(i * LANES, (i + 1) * LANES)
        row_stack[0:padded, here] = high
        row_stack[padded:, here] = low
        high32, low32 = high.astype(F32), low.astype(F32)
        tall = jnp.concatenate(
            [high32, high32, low32, jnp.zeros((deep - 3 * padded, LANES), F32)], axis=0
        )
        row_turned[here, :] = (0.5 * tall.T).astype(BF16)


def turn(row_blocks, padded, deep):
    words = row_blocks.shape[0] * LANES
    return pl.pallas_call(
        turn_kernel,
        name="turn_rows",
        in_specs=whole(1),
        out_specs=whole(2),
        out_shape=[
            jax.ShapeDtypeStruct((2 * padded, words), BF16),
            jax.ShapeDtypeStruct((words, deep), BF16),
        ],
        compiler_params=pltpu.CompilerParams(vmem_limit_bytes=24 << 20),
    )(row_blocks)


def stack_kernel(core, col_blocks, *rest):
    out = rest[-1]
    dim = out.shape[0] // 2
    for i in range(col_blocks.shape[0]):
        high, low = split(taller(col_blocks[i, 0], dim))
        here = slice(i * LANES, (i + 1) * LANES)
        out[0:dim, here] = high
        out[dim:, here] = low


def stack_cols(core, col_blocks, padded, near, earlier=None):
    n_col, dim, _ = col_blocks.shape
    seats = n_col // CORES
    step = BLOCKS // 2
    first = 0 if earlier is None else seats // step // 2
    ready = [] if earlier is None else [earlier]
    col_blocks = pltpu.with_memory_space_constraint(col_blocks.reshape(seats, CORES, dim, LANES), pltpu.HBM)
    pick = lambda g, core: (first + g, core[0] if near else 1 - core[0], 0, 0)
    return pl.pallas_call(
        stack_kernel,
        name="stack_near" if near else "stack_far",
        grid_spec=pltpu.PrefetchScalarGridSpec(
            num_scalar_prefetch=1,
            grid=(seats // step // 2,),
            in_specs=[pl.BlockSpec((step, 1, dim, LANES), pick)]
            + [pl.BlockSpec(memory_space=pltpu.HBM)] * len(ready),
            out_specs=pl.BlockSpec((2 * padded, step * LANES), lambda g, *_: (0, first + g)),
        ),
        out_shape=pltpu.HBM((2 * padded, seats * LANES), BF16),
        input_output_aliases={2: 0} if ready else {},
        compiler_params=pltpu.CompilerParams(vmem_limit_bytes=14 << 20),
    )(core, col_blocks, *ready)


def part_kernel(
    order, spots, offsets, core, row_turned, row_stack, stack_far, counts_far, masses, *rest, near, first, merge
):
    merging = []
    if merge:
        *merging, rest = rest[1], rest[2], *rest[-2:], rest[:1] + rest[3:-2]
    if near:
        row_bias, col_bias, col_term, row_term, scores, grads, counts, stacks = rest[-10:-2]
    else:
        col_term, row_term, row_bias, col_bias, scores, grads, counts, stacks = rest[-10:-2]
    arrival, stack_arrivals = rest[-2:]
    padded, n_row = row_term.shape[1], row_term.shape[0]
    n_col = col_bias.shape[0]
    step = pl.program_id(0)
    ct = step + first
    half_chunks = n_col // CORES // BLOCKS
    side = core[0] if near else 1 - core[0]

    width = BLOCKS * LANES
    fetch = pltpu.make_async_copy(counts_far, counts, arrival)

    def bring(chunk):
        cols = pl.ds(pl.multiple_of((first + chunk) * width, width), width)
        kept = stacks.at[chunk, pl.ds(0, 2 * padded), :]
        return pltpu.make_async_copy(stack_far.at[:, cols], kept, stack_arrivals.at[chunk])

    @pl.when(step == 0)
    def _():
        if not near:
            bring(0).start()
            fetch.start()
            for chunk in range(1, stacks.shape[0]):
                bring(chunk).start()
        if not near:
            log_total = jnp.log(masses[n_col + n_row : n_col + n_row + 1, :])
            col_bias[...] = 0.5 * (jnp.log(masses[0:n_col, :]) - log_total)
            row_logs = 0.5 * jnp.log(masses[n_col : n_col + n_row, :])
            for i in range(n_row):
                turned = jnp.broadcast_to(row_logs[i : i + 1, :], (LANES, LANES)).T
                row_bias[i * LANES // 8 : (i + 1) * LANES // 8] = turned.reshape(-1, 8, LANES)
        row_term[...] = rest[0][...] if near else jnp.zeros(row_term.shape, F32)

    if near:
        stacks[step, 0 : 2 * padded, :] = stack_far[:, first * width : (first + 1) * width]
    else:
        bring(step).wait()
    stacks[step, 2 * padded : 3 * padded, :] = stacks[step, 0:padded, :]
    stacks[step, 3 * padded :, :] = jnp.zeros((stacks.shape[1] - 3 * padded, width), BF16)
    product = jnp.dot(row_turned[...], stacks[step], preferred_element_type=F32)
    for k in range(BLOCKS):
        bias = col_bias[pl.ds((ct * BLOCKS + k) * 2 + side, 1), :]
        value = product[:, k * LANES : (k + 1) * LANES].reshape(-1, 8, LANES) + row_bias[...] + bias
        scores[:, k] = value
        grads[:, k] = 0.5 * jnp.tanh(value) + 0.5
    here = ct + (half_chunks if near else 0)
    begin = offsets[here]
    end = offsets[here + 1]

    if not near:

        @pl.when(step == 0)
        def _():
            fetch.wait()

    def counted(group, carry):
        found = []
        for u in range(8):
            at = jnp.minimum(begin + group * 8 + u, end - 1)
            spot = spots[at]
            row, k = lax.shift_right_logical(spot, BLOCKS.bit_length() - 1), spot & (BLOCKS - 1)
            count = (counts_far if near else counts)[order[at]]
            fresh = (0.1 + 0.25 * jnp.sqrt(count)) * (2.0 * scores[row, k] - jnp.log(count))
            found.append((row, k, fresh))
        for row, k, fresh in found:
            grads[row, k] = fresh
        return carry

    lax.fori_loop(0, lax.shift_right_logical(end - begin + 7, 3), counted, 0)
    if merge:
        piece, swapped, merged, leaves = merging
        merged[0 : first * BLOCKS] = swapped[0 : first * BLOCKS] + piece[...]
        parts = [pl.ds(0, first * BLOCKS), pl.ds(first * BLOCKS, BLOCKS)]
        leave = [
            pltpu.make_async_copy(merged.at[part], col_term.at[part], leaves.at[i])
            for i, part in enumerate(parts)
        ]
        leave[0].start()
    pieces = [split(grads[:, k].reshape(-1, LANES)) for k in range(BLOCKS)]
    high = jnp.concatenate([piece[0] for piece in pieces], axis=1)
    low = jnp.concatenate([piece[1] for piece in pieces], axis=1)
    both = jnp.dot(row_stack[...], high, preferred_element_type=F32)
    rest_ = jnp.dot(row_stack[0:padded, :], low, preferred_element_type=F32)
    total = both[0:padded] + both[padded:] + rest_
    for k in range(BLOCKS):
        block = total[:, k * LANES : (k + 1) * LANES]
        if merge:
            merged[first * BLOCKS + k] = swapped[first * BLOCKS + k] + block
        else:
            col_term[k] = block
    if merge:
        leave[1].start()
    turned = (((1,), (1,)), ((), ()))
    both = lax.dot_general(stacks[step, 0 : 2 * padded, :], high, turned, preferred_element_type=F32)
    rest_ = lax.dot_general(stacks[step, 0:padded, :], low, turned, preferred_element_type=F32)
    total = both[0:padded] + both[padded:] + rest_
    for i in range(n_row):
        row_term[i] = row_term[i] + total[:, i * LANES : (i + 1) * LANES]
    if merge:
        for copy in leave:
            copy.wait()


def part_grads(scalars, row_turned, row_stack, col_stack, counts, masses, earlier, first, count, extra=()):
    words, deep = row_turned.shape
    padded = row_stack.shape[0] // 2
    blocks = col_stack.shape[1] // LANES
    near = earlier is not None
    merge = bool(extra)
    ready, biases = ([earlier[0]], list(earlier[1:])) if near else ([], [])
    placed = (col_stack, counts) if near else [pltpu.with_memory_space_constraint(value, pltpu.HBM) for value in (col_stack, counts)]
    out_blocks = blocks if merge else count * BLOCKS
    scratch = [
        pltpu.VMEM((blocks, padded, LANES), F32),
        pltpu.SemaphoreType.DMA((2,)),
    ]
    return pl.pallas_call(
        functools.partial(part_kernel, near=near, first=first, merge=merge),
        name="merge_grads" if merge else "near_grads" if near else "far_grads",
        grid_spec=pltpu.PrefetchScalarGridSpec(
            num_scalar_prefetch=4,
            grid=(count,),
            in_specs=whole(2)
            + [pl.BlockSpec(memory_space=pltpu.VMEM if near else pltpu.HBM)] * 2
            + whole(1 + len(ready) + len(extra) + len(biases)),
            out_specs=[
                pl.BlockSpec(memory_space=pltpu.HBM)
                if merge
                else pl.BlockSpec((BLOCKS, padded, LANES), lambda g, *_: (g, 0, 0)),
                pl.BlockSpec((words // LANES, padded, LANES), lambda g, *_: (0, 0, 0)),
            ]
            + whole(0 if near else 2),
            scratch_shapes=[
                pltpu.VMEM((words // 8, BLOCKS, 8, LANES), F32),
                pltpu.VMEM((words // 8, BLOCKS, 8, LANES), F32),
                pltpu.VMEM((8, 8, LANES) if near else counts.shape, F32),
                pltpu.VMEM((count, deep, BLOCKS * LANES), BF16),
                pltpu.SemaphoreType.DMA(()),
                pltpu.SemaphoreType.DMA((count,)),
            ]
            + (scratch if merge else []),
        ),
        out_shape=[
            (pltpu.HBM if merge else jax.ShapeDtypeStruct)((out_blocks, padded, LANES), F32),
            (pltpu.HBM if merge else jax.ShapeDtypeStruct)((words // LANES, padded, LANES), F32),
        ]
        + ([] if near else [jax.ShapeDtypeStruct((words // 8, 8, LANES), F32), jax.ShapeDtypeStruct((blocks * CORES, LANES), F32)]),
        compiler_params=pltpu.CompilerParams(vmem_limit_bytes=36 << 20),
    )(*scalars, row_turned, row_stack, *placed, masses, *ready, *extra, *biases)


def swap_sum(value, axis, size, bit):
    return value + lax.ppermute(value, axis, [(i, i ^ bit) for i in range(size)])


def per_device(blocks, plan, live, row_emb, col_emb, row_acc, col_acc):
    n_z = lax.axis_size("col")
    n_row_axis = GRID_X * GRID_Y * CORES
    dim, words = row_emb.shape
    padded = -(-dim // 16) * 16
    deep = -(-3 * padded // 256) * 256
    core = lax.axis_index("core").astype(jnp.int32).reshape(1)
    places = plan[0, 0]
    alive = lax.broadcasted_iota(jnp.int32, places.shape, 2) < live[0, 0][:, :, None]
    target = jnp.where(alive, places, places[:, :, :1]).reshape(-1)
    tile_rows, tile_cols = words * n_z, words * n_row_axis
    n_col, n_row = tile_cols // LANES, tile_rows // LANES
    order, spots, offsets = sort_slots(target, core, n_col)
    col_blocks = lax.all_gather(col_emb, ROW, axis=0)
    row_emb_late, col_blocks, order, spots, offsets = lax.optimization_barrier(
        (row_emb, col_blocks, order, spots, offsets)
    )
    row_blocks = lax.all_gather(row_emb_late, "col", axis=0)
    sub_rows, sub_cols = blocks.shape[5:]
    slots_each = blocks.shape[4]
    arrived = lax.all_to_all(
        blocks.reshape(-1, slots_each, sub_rows, sub_cols), ALL, split_axis=0, concat_axis=0, tiled=True
    ).reshape(-1, sub_rows, sub_cols)
    counts, part = place(
        pltpu.with_memory_space_constraint(target, pltpu.HBM), alive.astype(jnp.int32).reshape(-1), arrived, tile_rows // sub_rows, n_col
    )
    row_part = part[n_col:]
    row_part = swap_sum(row_part, "col", n_z, 1)
    row_part = swap_sum(row_part, "col", n_z, 2)
    row_part, col_blocks = lax.optimization_barrier((row_part, col_blocks))
    row_part = swap_sum(row_part, "col", n_z, 4)
    far_stack = stack_cols(core, col_blocks, padded, False)
    row_part, far_stack = lax.optimization_barrier((row_part, far_stack))
    col_part = jnp.concatenate([part[:n_col], row_part[n_row:]], axis=0)
    col_part = swap_sum(col_part, "core", CORES, 1)
    col_part, far_stack, col_blocks = lax.optimization_barrier((col_part, far_stack, col_blocks))
    col_part = swap_sum(col_part, "y", GRID_Y, 1)
    far_stack = stack_cols(core, col_blocks, padded, False, far_stack)
    col_part, far_stack, col_blocks = lax.optimization_barrier((col_part, far_stack, col_blocks))
    col_part = swap_sum(col_part, "y", GRID_Y, 2)
    near_stack = stack_cols(core, col_blocks, padded, True)
    col_part, near_stack, col_blocks = lax.optimization_barrier((col_part, near_stack, col_blocks))
    col_part = swap_sum(col_part, "x", GRID_X, 1)
    near_stack = stack_cols(core, col_blocks, padded, True, near_stack)
    col_part, near_stack = lax.optimization_barrier((col_part, near_stack))
    col_part, row_blocks = lax.optimization_barrier((col_part, row_blocks))
    row_stack, row_turned = turn(row_blocks, padded, deep)
    col_part = swap_sum(col_part, "x", GRID_X, 2)
    masses = jnp.concatenate([col_part[:n_col], row_part[:n_row], col_part[n_col:]], axis=0)
    scalars = (order, spots, offsets, core)
    chunks = n_col // CORES // BLOCKS
    early = chunks // 2
    inputs = (scalars, row_turned, row_stack)
    far_term, row_term, *biases = part_grads(*inputs, far_stack, counts, masses, None, 0, chunks)
    swapped = lax.ppermute(far_term, "core", [(0, 1), (1, 0)])
    piece, row_term = part_grads(*inputs, near_stack, counts, masses, (row_term, *biases), 0, early)
    half, row_term = part_grads(
        *inputs, near_stack, counts, masses, (row_term, *biases), early, chunks - early, (piece, swapped)
    )
    loss_scale = 4.0 * float(words * n_z * n_row_axis) ** (-0.5)
    row_grad = lax.psum_scatter(row_term, "col", scatter_dimension=0, tiled=False)
    arrived_cols = lax.all_to_all(half, ("x", "y"), split_axis=0, concat_axis=0, tiled=True)
    row_share = row_grad[:dim] * loss_scale
    new_row_acc = row_acc + row_share * row_share
    new_row_emb = row_emb - LEARNING_RATE * row_share / jnp.sqrt(new_row_acc)
    arrived_cols, new_row_acc, new_row_emb = lax.optimization_barrier((arrived_cols, new_row_acc, new_row_emb))
    col_share = jnp.sum(arrived_cols, axis=0)[:dim] * loss_scale
    new_col_acc = col_acc + col_share * col_share
    new_col_emb = col_emb - LEARNING_RATE * col_share / jnp.sqrt(new_col_acc)
    return (new_row_emb, new_col_emb, new_row_acc, new_col_acc)

def solution(mesh):
    n_z = mesh.devices.shape[1]
    inner = Mesh(mesh.devices.reshape(GRID_X, GRID_Y, CORES, n_z), ROW + ("col",))
    row_words = P(None, ROW + ("col",))
    col_words = P(None, ("col",) + ROW)
    return jax.shard_map(
        per_device,
        mesh=inner,
        in_specs=(P(ROW, "col"), P(ROW, "col"), P(ROW, "col"), row_words, col_words, row_words, col_words),
        out_specs=(row_words, col_words, row_words, col_words),
        check_vma=False,
    )
```
